32 devices in a mesh: row: 4 (over z), col: 8 (over y, x, core).
Axes of the slice: x: 2, y: 2, z: 4, core: 2. Of those that a mesh axis runs over, the one named last changes fastest.
Arguments:
- features: bfloat16 [32, 64, 1024], P('row', 'col'), may hold values from -6 to 6
- gate_branch: bfloat16 [32, 64, 1024], P('row', 'col'), may hold values from -6 to 6
- w_row_proj: bfloat16 [1024, 128], replicated, may hold values from -0.1875 to 0.1875
- w_dt_row: bfloat16 [2, 32, 1024], P(None, None, 'col'), may hold values from -1 to 1
- dt_bias_row: float32 [2, 1024], P(None, 'col'), may hold values from -5 to -1
- rate_row: float32 [2, 1024, 16], P(None, 'col'), may hold values from 0.01 to 1
- skip_row: float32 [1024], P('col'), may hold values from 0.5 to 1.5
- conv_kernel: float32 [3, 3, 1024], P(None, None, 'col'), may hold values from -2 to 2
- conv_bias: float32 [1024], P('col'), may hold values from -3 to 3
- w_col_proj: bfloat16 [1024, 128], replicated, may hold values from -0.1875 to 0.1875
- w_dt_col: bfloat16 [2, 32, 1024], P(None, None, 'row'), may hold values from -1 to 1
- dt_bias_col: float32 [2, 1024], P(None, 'row'), may hold values from -5 to -1
- rate_col: float32 [2, 1024, 16], P(None, 'row'), may hold values from 0.01 to 1
Outputs:
- block_out: bfloat16 [32, 64, 1024], P(None, 'col', 'row')
The draws below stay inside these ranges and needn't reach their ends.
All inputs are finite; a program needn't handle non-finite values.
Results may differ from the reference program's by a relative error of at most 0.0085.
The reference program's roundings to bfloat16 on the way (of `row_proj`, `gated_rows`, `mixed_cells` and `col_proj`) count: a program that leaves them out, or rounds other values in their place, can miss the bound.
Values may be sent and summed in bfloat16 or wider, within the bound.
No kernel may reach another device: no remote copies, remote signals or barrier semaphores. Data moves between devices by JAX's collectives and lax.ppermute only.
A program may use at most 64 MiB of HBM per device.

```python
import math
import jax
import jax.numpy as jnp
from jax import lax

E = 1024
STATE = 16
RANK = 32
PROJ = 128
H = 32
W = 64


def block_scale(stream_key, shape, split, low, largest):
    factor_of, own = 1.0, jax.random.fold_in(stream_key, 6)
    for axis_at, blocks in split:
        heights = jnp.exp(jax.random.uniform(jax.random.fold_in(own, axis_at), (blocks,), jnp.float32, low / len(split), largest / len(split)))
        factor_of = factor_of * jnp.repeat(heights, shape[axis_at] // blocks).reshape([-1 if axis == axis_at else 1 for axis in range(len(shape))])
    return factor_of


def noise(rng, extent, deviation, most, pieces=(), held_as=jnp.bfloat16):
    entries = jax.random.normal(rng, extent, jnp.float32) * deviation
    if len(pieces) > 0:
        entries = block_scale(rng, extent, pieces, -0.22, 0.18) * entries
    return jnp.clip(entries, min=-most, max=most).astype(held_as)


def setup_inputs(seed: int = 0) -> dict:
    arg_keys = jax.random.split(jax.random.key(seed), 14)
    return {
        "features": noise(arg_keys[0], (H, W, E), 1.0, 6.0, ((0, 4), (1, 8))),
        "gate_branch": noise(arg_keys[1], (H, W, E), 1.0, 6.0, ((0, 4), (1, 8))),
        "w_row_proj": noise(arg_keys[2], (E, PROJ), E ** -0.5, 0.1875),
        "w_dt_row": noise(arg_keys[3], (2, RANK, E), RANK ** -0.5, 1.0, ((2, 8),)),
        "dt_bias_row": jnp.clip(-5.0 + 4.0 * jax.random.uniform(arg_keys[4], (2, E), jnp.float32) ** block_scale(arg_keys[4], (2, E), ((1, 8),), -0.2, 0.2), -5.0, -1.0),
        "rate_row": jnp.clip(jnp.exp(math.log(1.0) - 4.6051702 * jax.random.uniform(arg_keys[5], (2, E, STATE), jnp.float32) ** block_scale(arg_keys[5], (2, E, STATE), ((1, 8),), -0.2, 0.2)), 0.01, 1.0),
        "skip_row": jnp.clip(0.5 + 1.0 * jax.random.uniform(arg_keys[6], (E,), jnp.float32) ** block_scale(arg_keys[6], (E,), ((0, 8),), -0.2, 0.2), 0.5, 1.5),
        "conv_kernel": noise(arg_keys[7], (3, 3, E), 9 ** -0.5, 2.0, ((2, 8),), jnp.float32),
        "conv_bias": noise(arg_keys[8], (E,), 0.5, 3.0, ((0, 8),), jnp.float32),
        "w_col_proj": noise(arg_keys[9], (E, PROJ), E ** -0.5, 0.1875),
        "w_dt_col": noise(arg_keys[10], (2, RANK, E), RANK ** -0.5, 1.0, ((2, 4),)),
        "dt_bias_col": jnp.clip(-5.0 + 4.0 * jax.random.uniform(arg_keys[11], (2, E), jnp.float32) ** block_scale(arg_keys[11], (2, E), ((1, 4),), -0.2, 0.2), -5.0, -1.0),
        "rate_col": jnp.clip(jnp.exp(math.log(1.0) - 4.6051702 * jax.random.uniform(arg_keys[12], (2, E, STATE), jnp.float32) ** block_scale(arg_keys[12], (2, E, STATE), ((1, 4),), -0.2, 0.2)), 0.01, 1.0),
    }


def line_scan(inputs, step_sizes, drive_in, read_out, decay_rates, reverse):
    if reverse:
        inputs = jnp.flip(inputs, 1)
        step_sizes = jnp.flip(step_sizes, 1)
        drive_in = jnp.flip(drive_in, 1)
        read_out = jnp.flip(read_out, 1)
    line_count = inputs.shape[0]
    channels = inputs.shape[2]
    state_width = drive_in.shape[2]

    def advance(carried, slices):
        current, step_now, b_now, c_now = slices
        carried = jnp.exp(-step_now[:, :, None] * decay_rates[None]) * carried + (step_now * current)[:, :, None] * b_now[:, None, :]
        return carried, jnp.sum(carried * c_now[:, None, :], axis=2)

    initial = jnp.zeros((line_count, channels, state_width), jnp.float32)
    sequence = (jnp.swapaxes(inputs, 0, 1), jnp.swapaxes(step_sizes, 0, 1), jnp.swapaxes(drive_in, 0, 1), jnp.swapaxes(read_out, 0, 1))
    last_state, outputs = lax.scan(advance, initial, sequence)
    outputs = jnp.swapaxes(outputs, 0, 1)
    if reverse:
        outputs = jnp.flip(outputs, 1)
    return outputs


def both_ways(values, projections, step_weight, step_bias, decay_rates, skip_gain):
    low_rank = step_weight.shape[1]
    state_width = decay_rates.shape[2]
    segment = low_rank + 2 * state_width
    line_count = values.shape[0]
    positions = values.shape[1]
    if skip_gain is None:
        summed = jnp.zeros(values.shape, jnp.float32)
    else:
        summed = skip_gain * values
    for direction in range(2):
        offset = direction * segment
        low_part = projections[:, :, offset:offset + low_rank]
        raw_steps = jnp.dot(low_part.reshape(-1, low_rank), step_weight[direction], preferred_element_type=jnp.float32)
        raw_steps = raw_steps.reshape(line_count, positions, -1)
        step_sizes = jax.nn.softplus(raw_steps + step_bias[direction])
        drive_in = projections[:, :, offset + low_rank:offset + low_rank + state_width].astype(jnp.float32)
        read_out = projections[:, :, offset + low_rank + state_width:offset + segment].astype(jnp.float32)
        summed = summed + line_scan(values, step_sizes, drive_in, read_out, decay_rates[direction], direction == 1)
    return summed


def reference(features, gate_branch, w_row_proj, w_dt_row, dt_bias_row, rate_row, skip_row, conv_kernel, conv_bias, w_col_proj, w_dt_col, dt_bias_col, rate_col):
    height, width_all, channels_all = features.shape
    row_proj = jnp.dot(features.reshape(-1, channels_all), w_row_proj, preferred_element_type=jnp.float32)
    row_proj = row_proj.astype(jnp.bfloat16).reshape(height, width_all, -1)
    row_mix = both_ways(features.astype(jnp.float32), row_proj, w_dt_row, dt_bias_row, rate_row, skip_row)
    gated_rows = (row_mix * jax.nn.silu(gate_branch.astype(jnp.float32))).astype(jnp.bfloat16)
    padded = jnp.pad(gated_rows.astype(jnp.float32), ((1, 1), (1, 1), (0, 0)))
    accumulated = jnp.zeros((height, width_all, channels_all), jnp.float32) + conv_bias
    for vertical in range(3):
        for lateral in range(3):
            accumulated = accumulated + conv_kernel[vertical, lateral] * padded[vertical:vertical + height, lateral:lateral + width_all]
    mixed_cells = jax.nn.silu(accumulated).astype(jnp.bfloat16)
    col_proj = jnp.dot(mixed_cells.reshape(-1, channels_all), w_col_proj, preferred_element_type=jnp.float32)
    col_proj = col_proj.astype(jnp.bfloat16).reshape(height, width_all, -1)
    column_out = both_ways(jnp.swapaxes(mixed_cells.astype(jnp.float32), 0, 1), jnp.swapaxes(col_proj, 0, 1), w_dt_col, dt_bias_col, rate_col, None)
    return jnp.swapaxes(column_out, 0, 1).astype(jnp.bfloat16)
```

```python
import functools
import math

import jax
import jax.numpy as jnp
from jax import lax
from jax.experimental import pallas as pl
from jax.experimental.pallas import tpu as pltpu
from jax.sharding import PartitionSpec as P

LANES = 128
F32 = jnp.float32
BF16 = jnp.bfloat16
LOG2E = math.log2(math.e)


def dot(a, b):
    return jnp.dot(a, b, preferred_element_type=F32)


def silu(v):
    return v / (1.0 + jnp.exp(-v))


def softplus(v):
    return jnp.maximum(v, 0.0) + jnp.log1p(jnp.exp(-jnp.abs(v)))


def shuffle(tokens, outer, inner):
    shape = (tokens, tokens)
    to = lax.broadcasted_iota(jnp.int32, shape, 0).astype(F32)
    frm = lax.broadcasted_iota(jnp.int32, shape, 1).astype(F32)
    high = jnp.floor((to + 0.5) / inner)
    wanted = jnp.where(to < outer * inner, (to - high * inner) * outer + high, to)
    return jnp.where(frm == wanted, 1.0, 0.0).astype(BF16)


def pack_kernel(feat_ref, gate_ref, w_ref, out_ref):
    rows, cols, channels = feat_ref.shape
    tokens = rows * cols
    parts = out_ref.shape[0]
    share = channels // parts
    feats = feat_ref[...].reshape(tokens, channels)
    gates = gate_ref[...].reshape(tokens, channels)
    proj = dot(feats, w_ref[...]).astype(BF16)
    order = shuffle(tokens, cols, rows)
    feats = dot(order, feats).astype(BF16)
    gates = dot(order, gates).astype(BF16)
    proj = dot(order, proj).astype(BF16)
    for part in range(parts):
        out_ref[part, :, :share] = feats[:, part * share : (part + 1) * share]
        out_ref[part, :, share : 2 * share] = gates[:, part * share : (part + 1) * share]
        out_ref[part, :, 2 * share :] = proj


def prepare(proj, w_dt_ref, bias_ref, rate_ref, wide_ref, step_ref, rates_ref):
    _, rank, channels = w_dt_ref.shape
    state = rate_ref.shape[2]
    segment = rank + 2 * state
    lines = rates_ref.shape[2]
    wide_ref[...] = jnp.zeros_like(wide_ref)
    for k in range(2):
        wide_ref[pl.ds(k * segment, rank), pl.ds(k * channels, channels)] = w_dt_ref[k]
    raw = dot(proj, wide_ref[...])
    for k in range(2):
        part = raw[:, k * channels : (k + 1) * channels] + bias_ref[k : k + 1, :]
        step_ref[k] = softplus(part).reshape(step_ref.shape[1:])
        turned = jnp.transpose(rate_ref[k] * -LOG2E)
        for n in range(state):
            rates_ref[k, n] = jnp.broadcast_to(turned[n : n + 1, :], (lines, channels))


def scan(k, rank, step_ref, value_ref, proj_ref, rates_ref, out_ref, unroll):
    positions, lines, channels = out_ref.shape
    state = rates_ref.shape[1]
    base = k * (rank + 2 * state) + rank

    def advance(at, carried):
        pos = at if k == 0 else positions - 1 - at
        step = step_ref[k, pos]
        drive = step * value_ref[pos]
        proj = proj_ref[pos]
        total = out_ref[pos]
        states = []
        for n in range(state):
            b = jnp.broadcast_to(proj[:, base + n : base + n + 1], (lines, channels))
            c = jnp.broadcast_to(proj[:, base + state + n : base + state + n + 1], (lines, channels))
            s = jnp.exp2(step * rates_ref[k, n]) * carried[n] + drive * b
            states.append(s)
            total = total + c * s
        out_ref[pos] = total
        return tuple(states)

    zero = jnp.zeros((lines, channels), F32)
    lax.fori_loop(0, positions, advance, (zero,) * state, unroll=unroll)


def row_kernel(
    got_ref, w_dt_ref, bias_ref, rate_ref, skip_ref, out_ref, tail_ref,
    wide_ref, step_ref, rates_ref, value_ref, proj_ref, sum_ref, flat_ref,
):
    positions, lines, share = out_ref.shape
    rank = w_dt_ref.shape[1]
    width = got_ref.shape[2] - 2 * share
    proj = got_ref[:, :, 2 * share :].reshape(positions * lines, width)
    prepare(proj, w_dt_ref, bias_ref, rate_ref, wide_ref, step_ref, rates_ref)
    proj_ref[...] = proj.astype(F32).reshape(proj_ref.shape)
    values = got_ref[:, :, :share].astype(F32)
    value_ref[...] = values
    sum_ref[...] = values * skip_ref[...]
    for k in range(2):
        scan(k, rank, step_ref, value_ref, proj_ref, rates_ref, sum_ref, 4)
    gated = sum_ref[...] * silu(got_ref[:, :, share : 2 * share].astype(F32))
    out_ref[...] = gated.astype(BF16)
    flat_ref[...] = gated.reshape(flat_ref.shape)
    for j in range(2):
        tail_ref[j] = flat_ref[pl.ds(lines - 2 + j, positions, stride=lines), :].astype(BF16)


def conv_kernel(mid_ref, above_ref, taps_ref, bias_ref, out_ref, pad_ref, low_ref):
    positions, lines, share = mid_ref.shape
    parts = out_ref.shape[0]
    cols = positions // parts
    mid = mid_ref[...].astype(F32)
    zero_edge = jnp.zeros((1, lines + 8, share), F32)
    pad_ref[0:1] = zero_edge
    pad_ref[positions + 1 : positions + 2] = zero_edge
    pad_ref[1 : positions + 1, 8 : 8 + lines, :] = mid
    above = above_ref[...].astype(F32)
    pad_ref[1 : positions + 1, 6:7, :] = above[0][:, None, :]
    pad_ref[1 : positions + 1, 7:8, :] = above[1][:, None, :]
    total = jnp.zeros((positions, lines, share), F32) + bias_ref[...]
    for i in range(3):
        for j in range(3):
            total = total + taps_ref[i, j : j + 1, :] * pad_ref[j : j + positions, 6 + i : 6 + i + lines, :]
    main = silu(total).astype(BF16)
    out_ref[:, : cols * lines, :] = main.reshape(parts, cols * lines, share)
    low_ref[...] = jnp.zeros_like(low_ref)
    for j in range(2):
        low_ref[j, 8 : 8 + positions, :] = mid[:, lines - 2 + j, :]
    last = jnp.zeros((positions, share), F32) + bias_ref[...]
    for i in range(2):
        for j in range(3):
            last = last + taps_ref[i, j : j + 1, :] * low_ref[i, 7 + j : 7 + j + positions, :]
    out_ref[:, cols * lines :, :] = silu(last).astype(BF16).reshape(parts, cols, share)


def turn_kernel(me_ref, got_ref, w_ref, *out_refs, rows):
    parts, tokens, share = got_ref.shape
    width = w_ref.shape[1]
    count = len(out_refs)
    each = parts // count
    cols = tokens // (rows + 1)
    order = shuffle(tokens, rows, cols)
    total = jnp.zeros((tokens, width), F32)
    for part in range(parts):
        total = total + dot(got_ref[part], w_ref[pl.ds(part * share, share), :])
    proj = dot(order, total.astype(BF16)).astype(BF16)
    me = me_ref[0]
    for shift in range(count):
        to = lax.rem(me + shift, count)
        for j in range(each):
            moved = dot(order, got_ref[to * each + j]).astype(BF16)
            out_refs[shift][:, j * share : (j + 1) * share] = moved
        out_refs[shift][:, each * share :] = proj


def col_kernel(me_ref, *refs, count, rows):
    got_refs = refs[:count]
    (w_dt_ref, bias_ref, rate_ref, out_ref, wide_ref, step_ref, rates_ref, all_ref, value_ref, proj_ref, sum_ref) = refs[count:]
    positions, lines, share = out_ref.shape
    rank = w_dt_ref.shape[1]
    block = rows * lines
    me = me_ref[0]
    for shift in range(count):
        frm = lax.rem(me + count - shift, count)
        all_ref[pl.ds(pl.multiple_of(frm * block, block), block), :] = got_refs[shift][:block, :]

        @pl.when(frm == count - 1)
        def _():
            all_ref[pl.ds(count * block, lines), :] = got_refs[shift][block:, :]

    everything = all_ref[lines:, :]
    proj = everything[:, share:]
    prepare(proj, w_dt_ref, bias_ref, rate_ref, wide_ref, step_ref, rates_ref)
    proj_ref[...] = proj.astype(F32).reshape(proj_ref.shape)
    value_ref[...] = everything[:, :share].astype(F32).reshape(value_ref.shape)
    sum_ref[...] = jnp.zeros_like(sum_ref)
    for k in range(2):
        scan(k, rank, step_ref, value_ref, proj_ref, rates_ref, sum_ref, 4)
    out_ref[...] = sum_ref[...].astype(BF16)


def vmem():
    return pl.BlockSpec(memory_space=pltpu.VMEM)


def smem():
    return pl.BlockSpec(memory_space=pltpu.SMEM)


def call(kernel, name, outs, scratch, *args, scalars=0):
    many = isinstance(outs, (list, tuple))
    return pl.pallas_call(
        kernel,
        name=name,
        out_shape=outs,
        in_specs=[smem()] * scalars + [vmem()] * (len(args) - scalars),
        out_specs=[vmem()] * len(outs) if many else vmem(),
        scratch_shapes=scratch,
        compiler_params=pltpu.CompilerParams(vmem_limit_bytes=56 << 20),
    )(*args)


def array(shape, dtype=BF16):
    return jax.ShapeDtypeStruct(shape, dtype)


def scan_scratch(positions, lines, channels, width, state):
    return [
        pltpu.VMEM((width, 2 * channels), BF16),
        pltpu.VMEM((2, positions, lines, channels), F32),
        pltpu.VMEM((2, state, lines, channels), F32),
    ]


def local(
    features, gate_branch, w_row_proj, w_dt_row, dt_bias_row, rate_row, skip_row,
    conv_taps, conv_bias, w_col_proj, w_dt_col, dt_bias_col, rate_col,
):
    rows, cols, channels = features.shape
    width = w_row_proj.shape[1]
    state = rate_row.shape[2]
    n_col, n_row = lax.axis_size("col"), lax.axis_size("row")
    share, col_share = channels // n_col, channels // n_row
    line, column = cols * n_col, rows * n_row
    tokens, more = rows * cols, (rows + 1) * cols

    sent = call(pack_kernel, "pack", array((n_col, tokens, 2 * share + width)), [], features, gate_branch, w_row_proj)
    got = lax.all_to_all(sent, "col", 0, 0, tiled=True)
    gated, tail = call(
        row_kernel,
        "row_scan",
        [array((line, rows, share)), array((2, line, share))],
        scan_scratch(line, rows, share, width, state)
        + [
            pltpu.VMEM((line, rows, share), F32),
            pltpu.VMEM((line, rows, width), F32),
            pltpu.VMEM((line, rows, share), F32),
            pltpu.VMEM((line * rows, share), F32),
        ],
        got.reshape(line, rows, 2 * share + width),
        w_dt_row,
        dt_bias_row,
        rate_row,
        skip_row.reshape(1, share),
    )
    above = lax.ppermute(tail, "row", [(i, i + 1) for i in range(n_row - 1)])
    sent = call(
        conv_kernel,
        "conv",
        array((n_col, more, share)),
        [pltpu.VMEM((line + 2, rows + 8, share), F32), pltpu.VMEM((2, line + 16, share), F32)],
        gated,
        above,
        conv_taps,
        conv_bias.reshape(1, share),
    )
    got = lax.all_to_all(sent, "col", 0, 0, tiled=True)
    me = lax.axis_index("row").astype(jnp.int32).reshape(1)
    pieces = call(
        functools.partial(turn_kernel, rows=rows),
        "turn",
        [array((more, col_share + width))] * n_row,
        [],
        me,
        got,
        w_col_proj,
        scalars=1,
    )
    pieces = [pieces[0]] + [
        lax.ppermute(pieces[s], "row", [(i, (i + s) % n_row) for i in range(n_row)]) for s in range(1, n_row)
    ]
    return call(
        functools.partial(col_kernel, count=n_row, rows=rows),
        "col_scan",
        array((column, cols, col_share)),
        scan_scratch(column, cols, col_share, width, state)
        + [
            pltpu.VMEM(((column + 1) * cols, col_share + width), BF16),
            pltpu.VMEM((column, cols, col_share), F32),
            pltpu.VMEM((column, cols, width), F32),
            pltpu.VMEM((column, cols, col_share), F32),
        ],
        me,
        *pieces,
        w_dt_col,
        dt_bias_col,
        rate_col,
        scalars=1,
    )


def solution(mesh):
    return jax.shard_map(
        local,
        mesh=mesh,
        in_specs=(
            P("row", "col", None),
            P("row", "col", None),
            P(),
            P(None, None, "col"),
            P(None, "col"),
            P(None, "col", None),
            P("col"),
            P(None, None, "col"),
            P("col"),
            P(),
            P(None, None, "row"),
            P(None, "row"),
            P(None, "row", None),
        ),
        out_specs=P(None, "col", "row"),
        check_vma=False,
    )
```

```python
import functools
import math

import jax
import jax.numpy as jnp
from jax import lax
from jax.experimental import pallas as pl
from jax.experimental.pallas import tpu as pltpu
from jax.sharding import PartitionSpec as P

LANES = 128
F32 = jnp.float32
BF16 = jnp.bfloat16
LOG2E = math.log2(math.e)


def dot(a, b):
    return jnp.dot(a, b, preferred_element_type=F32)


def silu(v):
    return v / (1.0 + jnp.exp(-v))


def softplus(v):
    return jnp.maximum(v, 0.0) + jnp.log1p(jnp.exp(-jnp.abs(v)))


def shuffle(tokens, outer, inner):
    shape = (tokens, tokens)
    to = lax.broadcasted_iota(jnp.int32, shape, 0).astype(F32)
    frm = lax.broadcasted_iota(jnp.int32, shape, 1).astype(F32)
    high = jnp.floor((to + 0.5) / inner)
    wanted = jnp.where(to < outer * inner, (to - high * inner) * outer + high, to)
    return jnp.where(frm == wanted, 1.0, 0.0).astype(BF16)


def pack_kernel(feat_ref, gate_ref, w_ref, out_ref):
    rows, cols, channels = feat_ref.shape
    tokens = rows * cols
    parts = out_ref.shape[0]
    share = channels // parts
    feats = feat_ref[...].reshape(tokens, channels)
    gates = gate_ref[...].reshape(tokens, channels)
    proj = dot(feats, w_ref[...]).astype(BF16)
    order = shuffle(tokens, cols, rows)
    feats = dot(order, feats).astype(BF16)
    gates = dot(order, gates).astype(BF16)
    proj = dot(order, proj).astype(BF16)
    for part in range(parts):
        out_ref[part, :, :share] = feats[:, part * share : (part + 1) * share]
        out_ref[part, :, share : 2 * share] = gates[:, part * share : (part + 1) * share]
        out_ref[part, :, 2 * share :] = proj


def one_hot(height, width, hit):
    row = lax.broadcasted_iota(jnp.int32, (height, width), 0)
    column = lax.broadcasted_iota(jnp.int32, (height, width), 1)
    return jnp.where(hit(row, column), 1.0, 0.0).astype(BF16)


def prepare(proj, w_dt_ref, bias_ref, rate_ref, wide_ref, step_ref, rates_ref, pick_ref, ends_ref):
    _, rank, channels = w_dt_ref.shape
    state = rate_ref.shape[1]
    segment = rank + 2 * state
    lines = rates_ref.shape[2]
    wide_ref[...] = jnp.zeros_like(wide_ref)
    for k in range(2):
        wide_ref[pl.ds(k * segment, rank), pl.ds(k * channels, channels)] = w_dt_ref[k]
    raw = dot(proj, wide_ref[...])
    for k in range(2):
        part = raw[:, k * channels : (k + 1) * channels] + bias_ref[k : k + 1, :]
        step_ref[k] = softplus(part).reshape(step_ref.shape[1:])
        turned = rate_ref[k] * -LOG2E
        for n in range(state):
            rates_ref[k, n] = jnp.broadcast_to(turned[n : n + 1, :], (lines, channels))
        base = k * segment + rank
        ends_ref[k] = dot(proj, one_hot(proj.shape[1], 2 * state, lambda r, c: r == c + base)).astype(BF16)
    for n in range(state):
        pick_ref[n] = one_hot(2 * state, 2 * LANES, lambda r, c: r == n + jnp.where(c < LANES, 0, state))


def scan(k, step_ref, value_ref, rates_ref, pick_ref, ends_ref, state_ref, out_ref):
    positions, lines, channels = out_ref.shape
    state = rates_ref.shape[1]
    width = min(channels, LANES)
    groups = [pl.ds(at, width) for at in range(0, channels, width)]
    size = math.gcd(positions, max(1, 64 // (lines * len(groups))))
    state_ref[...] = jnp.zeros_like(state_ref)

    def advance(at, _):
        first = at * size if k == 0 else positions - (at + 1) * size
        first = pl.multiple_of(first, size)
        order = list(range(size)) if k == 0 else list(reversed(range(size)))
        steps = [[step_ref[k, first + p, :, g] for g in groups] for p in range(size)]
        drives = [[steps[p][i] * value_ref[first + p, :, g] for i, g in enumerate(groups)] for p in range(size)]
        totals = [[out_ref[first + p, :, g] for g in groups] for p in range(size)]
        ends = ends_ref[k, pl.ds(pl.multiple_of(first * lines, size * lines), size * lines), :]
        for n in range(state):
            rates = [rates_ref[k, n, :, g] for g in groups]
            held = [state_ref[n, :, g] for g in groups]
            spread = dot(ends, pick_ref[n])
            for p in order:
                b = spread[p * lines : (p + 1) * lines, :width]
                c = spread[p * lines : (p + 1) * lines, LANES : LANES + width]
                for i in range(len(groups)):
                    held[i] = jnp.exp2(steps[p][i] * rates[i]) * held[i] + drives[p][i] * b
                    totals[p][i] = totals[p][i] + c * held[i]
            for i, g in enumerate(groups):
                state_ref[n, :, g] = held[i]
        for p in range(size):
            for i, g in enumerate(groups):
                out_ref[first + p, :, g] = totals[p][i]
        return 0

    lax.fori_loop(0, positions // size, advance, 0)


def row_kernel(
    got_ref, w_dt_ref, bias_ref, rate_ref, skip_ref, out_ref, tail_ref,
    wide_ref, step_ref, rates_ref, pick_ref, ends_ref, state_ref, value_ref, sum_ref, flat_ref,
):
    positions, lines, share = out_ref.shape
    width = got_ref.shape[2] - 2 * share
    proj = got_ref[:, :, 2 * share :].reshape(positions * lines, width)
    prepare(proj, w_dt_ref, bias_ref, rate_ref, wide_ref, step_ref, rates_ref, pick_ref, ends_ref)
    values = got_ref[:, :, :share].astype(F32)
    value_ref[...] = values
    sum_ref[...] = values * skip_ref[...]
    for k in range(2):
        scan(k, step_ref, value_ref, rates_ref, pick_ref, ends_ref, state_ref, sum_ref)
    gated = sum_ref[...] * silu(got_ref[:, :, share : 2 * share].astype(F32))
    out_ref[...] = gated.astype(BF16)
    flat_ref[...] = gated.reshape(flat_ref.shape)
    for j in range(2):
        tail_ref[j] = flat_ref[pl.ds(lines - 2 + j, positions, stride=lines), :].astype(BF16)


def conv_kernel(mid_ref, above_ref, taps_ref, bias_ref, out_ref, pad_ref, low_ref):
    positions, lines, share = mid_ref.shape
    parts = out_ref.shape[0]
    cols = positions // parts
    mid = mid_ref[...].astype(F32)
    zero_edge = jnp.zeros((1, lines + 8, share), F32)
    pad_ref[0:1] = zero_edge
    pad_ref[positions + 1 : positions + 2] = zero_edge
    pad_ref[1 : positions + 1, 8 : 8 + lines, :] = mid
    above = above_ref[...].astype(F32)
    pad_ref[1 : positions + 1, 6:7, :] = above[0][:, None, :]
    pad_ref[1 : positions + 1, 7:8, :] = above[1][:, None, :]
    total = jnp.zeros((positions, lines, share), F32) + bias_ref[...]
    for i in range(3):
        for j in range(3):
            total = total + taps_ref[i, j : j + 1, :] * pad_ref[j : j + positions, 6 + i : 6 + i + lines, :]
    main = silu(total).astype(BF16)
    out_ref[:, : cols * lines, :] = main.reshape(parts, cols * lines, share)
    low_ref[...] = jnp.zeros_like(low_ref)
    for j in range(2):
        low_ref[j, 8 : 8 + positions, :] = mid[:, lines - 2 + j, :]
    last = jnp.zeros((positions, share), F32) + bias_ref[...]
    for i in range(2):
        for j in range(3):
            last = last + taps_ref[i, j : j + 1, :] * low_ref[i, 7 + j : 7 + j + positions, :]
    out_ref[:, cols * lines :, :] = silu(last).astype(BF16).reshape(parts, cols, share)


def turn_kernel(me_ref, got_ref, w_ref, *out_refs, rows):
    parts, tokens, share = got_ref.shape
    width = w_ref.shape[1]
    count = len(out_refs)
    each = parts // count
    cols = tokens // (rows + 1)
    order = shuffle(tokens, rows, cols)
    total = jnp.zeros((tokens, width), F32)
    for part in range(parts):
        total = total + dot(got_ref[part], w_ref[pl.ds(part * share, share), :])
    proj = dot(order, total.astype(BF16)).astype(BF16)
    me = me_ref[0]
    for shift in range(count):
        to = lax.rem(me + shift, count)
        for j in range(each):
            moved = dot(order, got_ref[to * each + j]).astype(BF16)
            out_refs[shift][:, j * share : (j + 1) * share] = moved
        out_refs[shift][:, each * share :] = proj


def col_kernel(me_ref, *refs, count, rows):
    got_refs = refs[:count]
    (w_dt_ref, bias_ref, rate_ref, out_ref, wide_ref, step_ref, rates_ref, pick_ref, ends_ref, state_ref, all_ref, value_ref, sum_ref) = refs[count:]
    positions, lines, share = out_ref.shape
    block = rows * lines
    me = me_ref[0]
    for shift in range(count):
        frm = lax.rem(me + count - shift, count)
        all_ref[pl.ds(pl.multiple_of(frm * block, block), block), :] = got_refs[shift][:block, :]

        @pl.when(frm == count - 1)
        def _():
            all_ref[pl.ds(count * block, lines), :] = got_refs[shift][block:, :]

    everything = all_ref[lines:, :]
    proj = everything[:, share:]
    prepare(proj, w_dt_ref, bias_ref, rate_ref, wide_ref, step_ref, rates_ref, pick_ref, ends_ref)
    value_ref[...] = everything[:, :share].astype(F32).reshape(value_ref.shape)
    sum_ref[...] = jnp.zeros_like(sum_ref)
    for k in range(2):
        scan(k, step_ref, value_ref, rates_ref, pick_ref, ends_ref, state_ref, sum_ref)
    out_ref[...] = sum_ref[...].astype(BF16)


def vmem():
    return pl.BlockSpec(memory_space=pltpu.VMEM)


def smem():
    return pl.BlockSpec(memory_space=pltpu.SMEM)


def call(kernel, name, outs, scratch, *args, scalars=0):
    many = isinstance(outs, (list, tuple))
    return pl.pallas_call(
        kernel,
        name=name,
        out_shape=outs,
        in_specs=[smem()] * scalars + [vmem()] * (len(args) - scalars),
        out_specs=[vmem()] * len(outs) if many else vmem(),
        scratch_shapes=scratch,
        compiler_params=pltpu.CompilerParams(vmem_limit_bytes=56 << 20),
    )(*args)


def array(shape, dtype=BF16):
    return pltpu.VMEM(shape, dtype)


def near(x):
    return pltpu.with_memory_space_constraint(x, pltpu.VMEM)


def scan_scratch(positions, lines, channels, width, state):
    return [
        pltpu.VMEM((width, 2 * channels), BF16),
        pltpu.VMEM((2, positions, lines, channels), F32),
        pltpu.VMEM((2, state, lines, channels), F32),
        pltpu.VMEM((state, 2 * state, 2 * LANES), BF16),
        pltpu.VMEM((2, positions * lines, 2 * state), BF16),
        pltpu.VMEM((state, lines, channels), F32),
    ]


def local(
    features, gate_branch, w_row_proj, w_dt_row, dt_bias_row, rate_row, skip_row,
    conv_taps, conv_bias, w_col_proj, w_dt_col, dt_bias_col, rate_col,
):
    rows, cols, channels = features.shape
    width = w_row_proj.shape[1]
    state = rate_row.shape[2]
    n_col, n_row = lax.axis_size("col"), lax.axis_size("row")
    share, col_share = channels // n_col, channels // n_row
    line, column = cols * n_col, rows * n_row
    tokens, more = rows * cols, (rows + 1) * cols

    sent = call(pack_kernel, "pack", array((n_col, tokens, 2 * share + width)), [], features, gate_branch, w_row_proj)
    got = lax.all_to_all(sent, "col", 0, 0, tiled=True)
    gated, tail = call(
        row_kernel,
        "row_scan",
        [array((line, rows, share)), array((2, line, share))],
        scan_scratch(line, rows, share, width, state)
        + [
            pltpu.VMEM((line, rows, share), F32),
            pltpu.VMEM((line, rows, share), F32),
            pltpu.VMEM((line * rows, share), F32),
        ],
        near(got.reshape(line, rows, 2 * share + width)),
        w_dt_row,
        dt_bias_row,
        jnp.swapaxes(rate_row, 1, 2),
        skip_row.reshape(1, share),
    )
    above = lax.ppermute(tail, "row", [(i, i + 1) for i in range(n_row - 1)])
    sent = call(
        conv_kernel,
        "conv",
        array((n_col, more, share)),
        [pltpu.VMEM((line + 2, rows + 8, share), F32), pltpu.VMEM((2, line + 16, share), F32)],
        near(gated),
        near(above),
        conv_taps,
        conv_bias.reshape(1, share),
    )
    got = lax.all_to_all(sent, "col", 0, 0, tiled=True)
    me = lax.axis_index("row").astype(jnp.int32).reshape(1)
    pieces = call(
        functools.partial(turn_kernel, rows=rows),
        "turn",
        [array((more, col_share + width))] * n_row,
        [],
        me,
        near(got),
        w_col_proj,
        scalars=1,
    )
    pieces = [pieces[0]] + [
        lax.ppermute(pieces[s], "row", [(i, (i + s) % n_row) for i in range(n_row)]) for s in range(1, n_row)
    ]
    return call(
        functools.partial(col_kernel, count=n_row, rows=rows),
        "col_scan",
        jax.ShapeDtypeStruct((column, cols, col_share), BF16),
        scan_scratch(column, cols, col_share, width, state)
        + [
            pltpu.VMEM(((column + 1) * cols, col_share + width), BF16),
            pltpu.VMEM((column, cols, col_share), F32),
            pltpu.VMEM((column, cols, col_share), F32),
        ],
        me,
        *[near(piece) for piece in pieces],
        w_dt_col,
        dt_bias_col,
        jnp.swapaxes(rate_col, 1, 2),
        scalars=1,
    )


def solution(mesh):
    return jax.shard_map(
        local,
        mesh=mesh,
        in_specs=(
            P("row", "col", None),
            P("row", "col", None),
            P(),
            P(None, None, "col"),
            P(None, "col"),
            P(None, "col", None),
            P("col"),
            P(None, None, "col"),
            P("col"),
            P(),
            P(None, None, "row"),
            P(None, "row"),
            P(None, "row", None),
        ),
        out_specs=P(None, "col", "row"),
        check_vma=False,
    )
```

```python
import functools
import math

import jax
import jax.numpy as jnp
from jax import lax
from jax.experimental import pallas as pl
from jax.experimental.pallas import tpu as pltpu
from jax.sharding import PartitionSpec as P

LANES = 128
F32 = jnp.float32
BF16 = jnp.bfloat16
LOG2E = math.log2(math.e)


def dot(a, b):
    return jnp.dot(a, b, preferred_element_type=F32)


def silu(v):
    return v / (1.0 + jnp.exp(-v))


def softplus(v):
    return jnp.maximum(v, 0.0) + jnp.log1p(jnp.exp(-jnp.abs(v)))


def shuffle(tokens, outer, inner):
    shape = (tokens, tokens)
    to = lax.broadcasted_iota(jnp.int32, shape, 0).astype(F32)
    frm = lax.broadcasted_iota(jnp.int32, shape, 1).astype(F32)
    high = jnp.floor((to + 0.5) / inner)
    wanted = jnp.where(to < outer * inner, (to - high * inner) * outer + high, to)
    return jnp.where(frm == wanted, 1.0, 0.0).astype(BF16)


def pack_kernel(feat_ref, gate_ref, w_ref, out_ref):
    rows, cols, channels = feat_ref.shape
    tokens = rows * cols
    parts = out_ref.shape[0]
    share = channels // parts
    feats = feat_ref[...].reshape(tokens, channels)
    gates = gate_ref[...].reshape(tokens, channels)
    proj = dot(feats, w_ref[...]).astype(BF16)
    order = shuffle(tokens, cols, rows)
    feats = dot(order, feats).astype(BF16)
    gates = dot(order, gates).astype(BF16)
    proj = dot(order, proj).astype(BF16)
    for part in range(parts):
        out_ref[part, :, :share] = feats[:, part * share : (part + 1) * share]
        out_ref[part, :, share : 2 * share] = gates[:, part * share : (part + 1) * share]
        out_ref[part, :, 2 * share :] = proj


def one_hot(height, width, hit):
    row = lax.broadcasted_iota(jnp.int32, (height, width), 0)
    column = lax.broadcasted_iota(jnp.int32, (height, width), 1)
    return jnp.where(hit(row, column), 1.0, 0.0).astype(BF16)


def prepare(proj, w_dt_ref, bias_ref, rate_ref, wide_ref, step_ref, rates_ref, pick_ref, ends_ref):
    _, rank, channels = w_dt_ref.shape
    state = rate_ref.shape[1]
    segment = rank + 2 * state
    lines = rates_ref.shape[2]
    wide_ref[...] = jnp.zeros_like(wide_ref)
    for k in range(2):
        wide_ref[pl.ds(k * segment, rank), pl.ds(k * channels, channels)] = w_dt_ref[k]
    raw = dot(proj, wide_ref[...])
    for k in range(2):
        part = raw[:, k * channels : (k + 1) * channels] + bias_ref[k : k + 1, :]
        step_ref[k] = softplus(part).reshape(step_ref.shape[1:])
        turned = rate_ref[k] * -LOG2E
        for n in range(state):
            rates_ref[k, n] = jnp.broadcast_to(turned[n : n + 1, :], (lines, channels))
        base = k * segment + rank
        ends_ref[k] = dot(proj, one_hot(proj.shape[1], 2 * state, lambda r, c: r == c + base)).astype(BF16)
    for n in range(state):
        pick_ref[n] = one_hot(2 * state, 2 * LANES, lambda r, c: r == n + jnp.where(c < LANES, 0, state))


def scan(step_ref, value_ref, rates_ref, pick_ref, ends_ref, state_ref, out_ref, back_ref):
    positions, lines, channels = out_ref.shape
    state = rates_ref.shape[1]
    width = min(channels, LANES)
    groups = [pl.ds(at, width) for at in range(0, channels, width)]
    size = math.gcd(positions, max(1, 32 // (lines * len(groups))))
    blocks = positions // size
    state_ref[...] = jnp.zeros_like(state_ref)

    def advance(at, _):
        firsts = (pl.multiple_of(at * size, size), pl.multiple_of((blocks - 1 - at) * size, size))
        orders = (list(range(size)), list(reversed(range(size))))
        steps, drives, ends = [], [], []
        for k, first in enumerate(firsts):
            steps.append([[step_ref[k, first + p, :, g] for g in groups] for p in range(size)])
            drives.append([[steps[k][p][i] * value_ref[first + p, :, g] for i, g in enumerate(groups)] for p in range(size)])
            ends.append(ends_ref[k, pl.ds(pl.multiple_of(first * lines, size * lines), size * lines), :])
        totals = [[[None] * len(groups) for _ in range(size)] for _ in firsts]
        both = jnp.concatenate(ends, axis=0)
        for n in range(state):
            spread = dot(both, pick_ref[n])
            held = [[state_ref[k, n, :, g] for g in groups] for k in range(2)]
            rates = [[rates_ref[k, n, :, g] for g in groups] for k in range(2)]
            for at_p in range(size):
                for k in range(2):
                    p = orders[k][at_p]
                    row = (k * size + p) * lines
                    b = spread[row : row + lines, :width]
                    c = spread[row : row + lines, LANES : LANES + width]
                    for i in range(len(groups)):
                        held[k][i] = jnp.exp2(steps[k][p][i] * rates[k][i]) * held[k][i] + drives[k][p][i] * b
                        read = c * held[k][i]
                        totals[k][p][i] = read if n == 0 else totals[k][p][i] + read
            for k in range(2):
                for i, g in enumerate(groups):
                    state_ref[k, n, :, g] = held[k][i]
        for p in range(size):
            for i, g in enumerate(groups):
                out_ref[firsts[0] + p, :, g] = totals[0][p][i]
                back_ref[firsts[1] + p, :, g] = totals[1][p][i]
        return 0

    lax.fori_loop(0, blocks, advance, 0, unroll=math.gcd(blocks, 4))


def row_kernel(
    got_ref, w_dt_ref, bias_ref, rate_ref, skip_ref, out_ref, tail_ref,
    wide_ref, step_ref, rates_ref, pick_ref, ends_ref, state_ref, value_ref, sum_ref, back_ref, flat_ref,
):
    positions, lines, share = out_ref.shape
    width = got_ref.shape[2] - 2 * share
    proj = got_ref[:, :, 2 * share :].reshape(positions * lines, width)
    prepare(proj, w_dt_ref, bias_ref, rate_ref, wide_ref, step_ref, rates_ref, pick_ref, ends_ref)
    value_ref[...] = got_ref[:, :, :share].astype(F32)
    scan(step_ref, value_ref, rates_ref, pick_ref, ends_ref, state_ref, sum_ref, back_ref)
    mix = sum_ref[...] + back_ref[...] + skip_ref[...] * value_ref[...]
    gated = mix * silu(got_ref[:, :, share : 2 * share].astype(F32))
    out_ref[...] = gated.astype(BF16)
    flat_ref[...] = gated.reshape(flat_ref.shape)
    for j in range(2):
        tail_ref[j] = flat_ref[pl.ds(lines - 2 + j, positions, stride=lines), :].astype(BF16)


def conv_kernel(me_ref, mid_ref, above_ref, taps_ref, bias_ref, out_ref, pad_ref):
    positions, lines, share = mid_ref.shape
    parts = out_ref.shape[0]
    cols = positions // parts
    height = pad_ref.shape[1]
    top = height - lines
    zero_edge = jnp.zeros((1, height, share), F32)
    pad_ref[0:1] = zero_edge
    pad_ref[positions + 1 : positions + 2] = zero_edge
    pad_ref[1 : positions + 1, top:, :] = mid_ref[...].astype(F32)
    flat_ref = pad_ref.reshape((positions + 2) * height, share)
    for j in range(2):
        flat_ref[pl.ds(height + top - 2 + j, positions, stride=height), :] = above_ref[j].astype(F32)
    slot = lax.broadcasted_iota(jnp.int32, (lines, share), 0)
    first = me_ref[0] == 0
    beyond = (jnp.logical_and(first, slot == 1), None, jnp.logical_and(first, slot == 0))
    taps = []
    for i in range(3):
        wide = [jnp.broadcast_to(taps_ref[i, j : j + 1, :], (lines, share)) for j in range(3)]
        taps.append(wide if beyond[i] is None else [jnp.where(beyond[i], 0.0, tap) for tap in wide])
    bias = jnp.broadcast_to(bias_ref[...], (lines, share))

    def block(part, _):
        start = part * cols
        for w in range(cols):
            total = bias
            for i in range(3):
                for j in range(3):
                    total = total + taps[i][j] * pad_ref[start + w + j, top - 2 + i : top - 2 + i + lines, :]
            out_ref[part, w * lines : (w + 1) * lines, :] = silu(total).astype(BF16)
        return 0

    lax.fori_loop(0, parts, block, 0, unroll=2)


def turn_kernel(me_ref, got_ref, w_ref, *out_refs, rows):
    parts, tokens, share = got_ref.shape
    width = w_ref.shape[1]
    count = len(out_refs)
    each = parts // count
    order = shuffle(tokens, rows, tokens // rows)
    total = jnp.zeros((tokens, width), F32)
    for part in range(parts):
        total = total + dot(got_ref[part], w_ref[pl.ds(part * share, share), :])
    proj = dot(order, total.astype(BF16)).astype(BF16)
    me = me_ref[0]
    for shift in range(count):
        to = lax.rem(me + shift, count)
        for j in range(each):
            moved = dot(order, got_ref[to * each + j]).astype(BF16)
            out_refs[shift][:, j * share : (j + 1) * share] = moved
        out_refs[shift][:, each * share :] = proj


def col_kernel(
    me_ref, *refs, count, rows,
):
    got_refs = refs[:count]
    (w_dt_ref, bias_ref, rate_ref, out_ref, wide_ref, step_ref, rates_ref, pick_ref, ends_ref,
     state_ref, proj_ref, value_ref, sum_ref, back_ref) = refs[count:]
    positions, lines, share = out_ref.shape
    block = rows * lines
    me = me_ref[0]
    for shift in range(count):
        frm = lax.rem(me + count - shift, count)
        piece = got_refs[shift][:, :share].astype(F32).reshape(rows, lines, share)
        value_ref[pl.ds(frm * rows, rows)] = piece
        proj_ref[pl.ds(pl.multiple_of(frm * block, block), block), :] = got_refs[shift][:, share:]

        @pl.when(frm == 0)
        def _():
            value_ref[positions] = piece[0]
            proj_ref[pl.ds(positions * lines, lines), :] = got_refs[shift][:lines, share:]

    proj = proj_ref[lines:, :]
    prepare(proj, w_dt_ref, bias_ref, rate_ref, wide_ref, step_ref, rates_ref, pick_ref, ends_ref)
    values = value_ref.at[pl.ds(1, positions)]
    scan(step_ref, values, rates_ref, pick_ref, ends_ref, state_ref, sum_ref, back_ref)
    out_ref[...] = (sum_ref[...] + back_ref[...]).astype(BF16)


def vmem():
    return pl.BlockSpec(memory_space=pltpu.VMEM)


def smem():
    return pl.BlockSpec(memory_space=pltpu.SMEM)


def call(kernel, name, outs, scratch, *args, scalars=0):
    many = isinstance(outs, (list, tuple))
    return pl.pallas_call(
        kernel,
        name=name,
        out_shape=outs,
        in_specs=[smem()] * scalars + [vmem()] * (len(args) - scalars),
        out_specs=[vmem()] * len(outs) if many else vmem(),
        scratch_shapes=scratch,
        compiler_params=pltpu.CompilerParams(vmem_limit_bytes=56 << 20),
    )(*args)


def array(shape, dtype=BF16):
    return pltpu.VMEM(shape, dtype)


def near(x):
    return pltpu.with_memory_space_constraint(x, pltpu.VMEM)


def scan_scratch(positions, lines, channels, width, state):
    return [
        pltpu.VMEM((width, 2 * channels), BF16),
        pltpu.VMEM((2, positions, lines, channels), F32),
        pltpu.VMEM((2, state, lines, channels), F32),
        pltpu.VMEM((state, 2 * state, 2 * LANES), BF16),
        pltpu.VMEM((2, positions * lines, 2 * state), BF16),
        pltpu.VMEM((2, state, lines, channels), F32),
    ]


def local(
    features, gate_branch, w_row_proj, w_dt_row, dt_bias_row, rate_row, skip_row,
    conv_taps, conv_bias, w_col_proj, w_dt_col, dt_bias_col, rate_col,
):
    rows, cols, channels = features.shape
    width = w_row_proj.shape[1]
    state = rate_row.shape[2]
    n_col, n_row = lax.axis_size("col"), lax.axis_size("row")
    share, col_share = channels // n_col, channels // n_row
    line, column = cols * n_col, rows * n_row
    tokens = rows * cols
    me = lax.axis_index("row").astype(jnp.int32).reshape(1)

    sent = call(pack_kernel, "pack", array((n_col, tokens, 2 * share + width)), [], features, gate_branch, w_row_proj)
    got = lax.all_to_all(sent, "col", 0, 0, tiled=True)
    gated, tail = call(
        row_kernel,
        "row_scan",
        [array((line, rows, share)), array((2, line, share))],
        scan_scratch(line, rows, share, width, state)
        + [
            pltpu.VMEM((line, rows, share), F32),
            pltpu.VMEM((line, rows, share), F32),
            pltpu.VMEM((line, rows, share), F32),
            pltpu.VMEM((line * rows, share), F32),
        ],
        near(got.reshape(line, rows, 2 * share + width)),
        near(w_dt_row),
        near(dt_bias_row),
        near(jnp.swapaxes(rate_row, 1, 2)),
        near(skip_row.reshape(1, share)),
    )
    above = lax.ppermute(tail, "row", [(i, (i + 1) % n_row) for i in range(n_row)])
    sent = call(
        conv_kernel,
        "conv",
        array((n_col, tokens, share)),
        [pltpu.VMEM((line + 2, rows + 8, share), F32)],
        me,
        near(gated),
        near(above),
        near(conv_taps),
        near(conv_bias.reshape(1, share)),
        scalars=1,
    )
    got = lax.all_to_all(sent, "col", 0, 0, tiled=True)
    pieces = call(
        functools.partial(turn_kernel, rows=rows),
        "turn",
        [array((tokens, col_share + width))] * n_row,
        [],
        me,
        near(got),
        near(w_col_proj),
        scalars=1,
    )
    pieces = [pieces[0]] + [
        lax.ppermute(pieces[s], "row", [(i, (i + s) % n_row) for i in range(n_row)]) for s in range(1, n_row)
    ]
    return call(
        functools.partial(col_kernel, count=n_row, rows=rows),
        "col_scan",
        jax.ShapeDtypeStruct((column, cols, col_share), BF16),
        scan_scratch(column, cols, col_share, width, state)
        + [
            pltpu.VMEM(((column + 1) * cols, width), BF16),
            pltpu.VMEM((column + 1, cols, col_share), F32),
            pltpu.VMEM((column, cols, col_share), F32),
            pltpu.VMEM((column, cols, col_share), F32),
        ],
        me,
        *[near(piece) for piece in pieces],
        near(w_dt_col),
        near(dt_bias_col),
        near(jnp.swapaxes(rate_col, 1, 2)),
        scalars=1,
    )


def solution(mesh):
    return jax.shard_map(
        local,
        mesh=mesh,
        in_specs=(
            P("row", "col", None),
            P("row", "col", None),
            P(),
            P(None, None, "col"),
            P(None, "col"),
            P(None, "col", None),
            P("col"),
            P(None, None, "col"),
            P("col"),
            P(),
            P(None, None, "row"),
            P(None, "row"),
            P(None, "row", None),
        ),
        out_specs=P(None, "col", "row"),
        check_vma=False,
    )
```

```python
import functools
import math

import jax
import jax.numpy as jnp
from jax import lax
from jax.experimental import pallas as pl
from jax.experimental.pallas import tpu as pltpu
from jax.sharding import PartitionSpec as P

LANES = 128
F32 = jnp.float32
BF16 = jnp.bfloat16
LOG2E = math.log2(math.e)


def dot(a, b):
    return jnp.dot(a, b, preferred_element_type=F32)


def silu(v):
    return v / (1.0 + jnp.exp(-v))


def softplus(v):
    return jnp.maximum(v, 0.0) + jnp.log1p(jnp.exp(-jnp.abs(v)))


def shuffle(tokens, outer, inner):
    shape = (tokens, tokens)
    to = lax.broadcasted_iota(jnp.int32, shape, 0).astype(F32)
    frm = lax.broadcasted_iota(jnp.int32, shape, 1).astype(F32)
    high = jnp.floor((to + 0.5) / inner)
    wanted = jnp.where(to < outer * inner, (to - high * inner) * outer + high, to)
    return jnp.where(frm == wanted, 1.0, 0.0).astype(BF16)


def fetches(sources, targets, sems):
    copies = [pltpu.make_async_copy(s, t, sems.at[i]) for i, (s, t) in enumerate(zip(sources, targets))]
    for copy in copies:
        copy.start()
    return copies


def pack_kernel(feat_hbm, gate_hbm, w_hbm, *refs):
    count = (len(refs) - 5) // 2
    param_refs, (out_ref, *held_refs) = refs[:count], refs[count : 2 * count + 1]
    feat_ref, gate_ref, w_ref, sems = refs[2 * count + 1 :]
    copies = fetches((feat_hbm, w_hbm, gate_hbm, *param_refs), (feat_ref, w_ref, gate_ref, *held_refs), sems)
    rows, cols, channels = feat_ref.shape
    tokens = rows * cols
    parts = out_ref.shape[0]
    share = channels // parts
    order = shuffle(tokens, cols, rows)
    copies[0].wait()
    feats = feat_ref[...].reshape(tokens, channels)
    moved = dot(order, feats).astype(BF16)
    for part in range(parts):
        out_ref[part, :, :share] = moved[:, part * share : (part + 1) * share]
    copies[1].wait()
    proj = dot(order, dot(feats, w_ref[...]).astype(BF16)).astype(BF16)
    for part in range(parts):
        out_ref[part, :, 2 * share :] = proj
    copies[2].wait()
    moved = dot(order, gate_ref[...].reshape(tokens, channels)).astype(BF16)
    for part in range(parts):
        out_ref[part, :, share : 2 * share] = moved[:, part * share : (part + 1) * share]
    for copy in copies[3:]:
        copy.wait()


def one_hot(height, width, hit):
    row = lax.broadcasted_iota(jnp.int32, (height, width), 0)
    column = lax.broadcasted_iota(jnp.int32, (height, width), 1)
    return jnp.where(hit(row, column), 1.0, 0.0).astype(BF16)


def prepare(proj, w_dt_ref, bias_ref, rate_ref, wide_ref, step_ref, rates_ref, pick_ref, ends_ref):
    _, rank, channels = w_dt_ref.shape
    state = rate_ref.shape[1]
    segment = rank + 2 * state
    lines = rates_ref.shape[2]
    wide_ref[...] = jnp.zeros_like(wide_ref)
    for k in range(2):
        wide_ref[pl.ds(k * segment, rank), pl.ds(k * channels, channels)] = w_dt_ref[k]
    raw = dot(proj, wide_ref[...])
    for k in range(2):
        part = raw[:, k * channels : (k + 1) * channels] + bias_ref[k : k + 1, :]
        step_ref[k] = softplus(part).reshape(step_ref.shape[1:])
        turned = rate_ref[k] * -LOG2E
        for n in range(state):
            rates_ref[k, n] = jnp.broadcast_to(turned[n : n + 1, :], (lines, channels))
        base = k * segment + rank
        ends_ref[k] = dot(proj, one_hot(proj.shape[1], 2 * state, lambda r, c: r == c + base)).astype(BF16)
    for n in range(state):
        pick_ref[n] = one_hot(2 * state, 2 * LANES, lambda r, c: r == n + jnp.where(c < LANES, 0, state))


def scan(step_ref, value_ref, rates_ref, pick_ref, ends_ref, state_ref, out_ref, back_ref):
    positions, lines, channels = out_ref.shape
    state = rates_ref.shape[1]
    width = min(channels, LANES)
    groups = [pl.ds(at, width) for at in range(0, channels, width)]
    size = math.gcd(positions, max(1, 32 // (lines * len(groups))))
    blocks = positions // size
    state_ref[...] = jnp.zeros_like(state_ref)

    def advance(at, _):
        firsts = (pl.multiple_of(at * size, size), pl.multiple_of((blocks - 1 - at) * size, size))
        orders = (list(range(size)), list(reversed(range(size))))
        steps, drives, ends = [], [], []
        for k, first in enumerate(firsts):
            steps.append([[step_ref[k, first + p, :, g] for g in groups] for p in range(size)])
            drives.append([[steps[k][p][i] * value_ref[first + p, :, g] for i, g in enumerate(groups)] for p in range(size)])
            ends.append(ends_ref[k, pl.ds(pl.multiple_of(first * lines, size * lines), size * lines), :])
        totals = [[[None] * len(groups) for _ in range(size)] for _ in firsts]
        both = jnp.concatenate(ends, axis=0)
        for n in range(state):
            spread = dot(both, pick_ref[n])
            held = [[state_ref[k, n, :, g] for g in groups] for k in range(2)]
            rates = [[rates_ref[k, n, :, g] for g in groups] for k in range(2)]
            for at_p in range(size):
                for k in range(2):
                    p = orders[k][at_p]
                    row = (k * size + p) * lines
                    b = spread[row : row + lines, :width]
                    c = spread[row : row + lines, LANES : LANES + width]
                    for i in range(len(groups)):
                        held[k][i] = jnp.exp2(steps[k][p][i] * rates[k][i]) * held[k][i] + drives[k][p][i] * b
                        read = c * held[k][i]
                        totals[k][p][i] = read if n == 0 else totals[k][p][i] + read
            for k in range(2):
                for i, g in enumerate(groups):
                    state_ref[k, n, :, g] = held[k][i]
        for p in range(size):
            for i, g in enumerate(groups):
                out_ref[firsts[0] + p, :, g] = totals[0][p][i]
                back_ref[firsts[1] + p, :, g] = totals[1][p][i]
        return 0

    lax.fori_loop(0, blocks, advance, 0, unroll=True)


def joint_scan(step_ref, value_ref, rates_ref, pick_ref, ends_ref, out_ref):
    positions, lines, channels = out_ref.shape
    state = rates_ref.shape[0]
    size = math.gcd(positions, 8)
    held = [jnp.zeros((lines, channels), F32)] * state
    for first in range(0, positions, size):
        steps = [step_ref[first + p] for p in range(size)]
        drives = [steps[p] * value_ref[first + p] for p in range(size)]
        totals = [None] * size
        ends = ends_ref[first * lines : (first + size) * lines, :]
        for n in range(state):
            spread = dot(ends, pick_ref[n])
            rates = rates_ref[n]
            for p in range(size):
                b = spread[p * lines : (p + 1) * lines, :channels]
                c = spread[p * lines : (p + 1) * lines, LANES : LANES + channels]
                held[n] = jnp.exp2(steps[p] * rates) * held[n] + drives[p] * b
                read = c * held[n]
                totals[p] = read if n == 0 else totals[p] + read
        for p in range(size):
            out_ref[first + p] = totals[p]


def row_tables(w_dt_ref, rate_ref, wide_ref, rates_ref, pick_ref):
    _, rank, channels = w_dt_ref.shape
    state = rate_ref.shape[1]
    segment = rank + 2 * state
    lines = rates_ref.shape[1]
    low = lax.broadcasted_iota(jnp.int32, (lines, channels), 0) < lines // 2
    wide_ref[...] = jnp.zeros_like(wide_ref)
    for k in range(2):
        wide_ref[pl.ds(k * segment, rank), pl.ds(k * channels, channels)] = w_dt_ref[k]
    turned = [rate_ref[k] * -LOG2E for k in range(2)]
    for n in range(state):
        rates_ref[n] = jnp.where(low, *[jnp.broadcast_to(t[n : n + 1, :], (lines, channels)) for t in turned])
        pick_ref[n] = one_hot(2 * state, 2 * LANES, lambda r, c: r == n + jnp.where(c < LANES, 0, state))


def half_rows(upper, rank, got_ref, bias_ref, skip_ref, wide_ref, rates_ref, pick_ref, out_ref, scratch):
    step_ref, value_ref, proj_ref, ends_ref, sum_ref = scratch
    positions, lines, share = out_ref.shape
    state = rates_ref.shape[0]
    segment = rank + 2 * state
    width = proj_ref.shape[2]
    half = lines // 2

    def low(columns):
        return lax.broadcasted_iota(jnp.int32, (lines, columns), 0) < half

    def swap(v):
        return pltpu.roll(v, half, 0)

    def packed(p, at):
        there = got_ref[p, :, at].astype(F32)
        back = got_ref[positions - 1 - p, :, at].astype(F32)
        there, back = (swap(there), back) if upper else (there, swap(back))
        return jnp.where(low(there.shape[1]), there, back)

    for p in range(positions):
        value_ref[p] = packed(p, pl.ds(0, share))
        proj_ref[p] = packed(p, pl.ds(2 * share, width))
    proj = proj_ref[...].reshape(positions * lines, width).astype(BF16)
    raw = dot(proj, wide_ref[...])
    parts = [(raw[:, k * share : (k + 1) * share] + bias_ref[k : k + 1, :]).reshape(positions, lines, share) for k in range(2)]
    step_ref[...] = softplus(jnp.where(low(share), *parts))
    ends = [
        dot(proj, one_hot(width, 2 * state, lambda r, c: r == c + k * segment + rank)).reshape(positions, lines, 2 * state)
        for k in range(2)
    ]
    ends_ref[...] = jnp.where(low(2 * state), *ends).reshape(ends_ref.shape).astype(BF16)
    joint_scan(step_ref, value_ref, rates_ref, pick_ref, ends_ref, sum_ref)
    for p in range(positions):
        there, back = sum_ref[p], sum_ref[positions - 1 - p]
        mix = swap(there) + back if upper else there + swap(back)
        mix = mix + skip_ref[...] * got_ref[p, :, :share].astype(F32)
        gated = mix * silu(got_ref[p, :, share : 2 * share].astype(F32))
        value_ref[p] = gated
        out_ref[p] = gated.astype(BF16)


def upper_kernel(got_ref, w_dt_ref, bias_ref, rate_ref, skip_ref, *refs):
    *scratch, sems = refs[-6:]
    count = (len(refs) - 11) // 2
    out_ref, tail_ref, wide_ref, rates_ref, pick_ref, *held_refs = refs[count:-6]
    copies = fetches(refs[:count], held_refs, sems)
    positions, lines, share = out_ref.shape
    row_tables(w_dt_ref, rate_ref, wide_ref, rates_ref, pick_ref)
    half_rows(True, w_dt_ref.shape[1], got_ref, bias_ref, skip_ref, wide_ref, rates_ref, pick_ref, out_ref, scratch)
    flat_ref = scratch[1].reshape(positions * lines, share)
    for j in range(2):
        tail_ref[j] = flat_ref[pl.ds(lines - 2 + j, positions, stride=lines), :].astype(BF16)
    for copy in copies:
        copy.wait()


def lower_kernel(got_ref, bias_ref, skip_ref, wide_ref, rates_ref, pick_ref, out_ref, *scratch, rank):
    half_rows(False, rank, got_ref, bias_ref, skip_ref, wide_ref, rates_ref, pick_ref, out_ref, scratch)


def conv_kernel(me_ref, lower_ref, upper_ref, above_ref, taps_ref, bias_ref, out_ref, pad_ref):
    positions, lines, share = lower_ref.shape
    parts = out_ref.shape[0]
    cols = positions // parts
    height = pad_ref.shape[1]
    top = height - lines
    zero_edge = jnp.zeros((1, height, share), F32)
    pad_ref[0:1] = zero_edge
    pad_ref[positions + 1 : positions + 2] = zero_edge
    slot = lax.broadcasted_iota(jnp.int32, (lines, share), 0)
    mid = jnp.where(slot < lines // 2, lower_ref[...].astype(F32), upper_ref[...].astype(F32))
    pad_ref[1 : positions + 1, top:, :] = mid
    flat_ref = pad_ref.reshape((positions + 2) * height, share)
    for j in range(2):
        flat_ref[pl.ds(height + top - 2 + j, positions, stride=height), :] = above_ref[j].astype(F32)
    first = me_ref[0] == 0
    beyond = (jnp.logical_and(first, slot == 1), None, jnp.logical_and(first, slot == 0))
    taps = []
    for i in range(3):
        wide = [jnp.broadcast_to(taps_ref[i, j : j + 1, :], (lines, share)) for j in range(3)]
        taps.append(wide if beyond[i] is None else [jnp.where(beyond[i], 0.0, tap) for tap in wide])
    bias = jnp.broadcast_to(bias_ref[...], (lines, share))

    def block(part, _):
        start = part * cols
        for w in range(cols):
            total = bias
            for i in range(3):
                for j in range(3):
                    total = total + taps[i][j] * pad_ref[start + w + j, top - 2 + i : top - 2 + i + lines, :]
            out_ref[part, w * lines : (w + 1) * lines, :] = silu(total).astype(BF16)
        return 0

    lax.fori_loop(0, parts, block, 0, unroll=2)


def turn_kernel(me_ref, got_ref, w_ref, *out_refs, rows):
    parts, tokens, share = got_ref.shape
    width = w_ref.shape[1]
    count = len(out_refs)
    each = parts // count
    order = shuffle(tokens, rows, tokens // rows)
    total = jnp.zeros((tokens, width), F32)
    for part in range(parts):
        total = total + dot(got_ref[part], w_ref[pl.ds(part * share, share), :])
    proj = dot(order, total.astype(BF16)).astype(BF16)
    me = me_ref[0]
    for shift in range(count):
        to = lax.rem(me + shift, count)
        for j in range(each):
            moved = dot(order, got_ref[to * each + j]).astype(BF16)
            out_refs[shift][:, j * share : (j + 1) * share] = moved
        out_refs[shift][:, each * share :] = proj


def col_kernel(
    me_ref, *refs, count, rows,
):
    got_refs = refs[:count]
    (w_dt_ref, bias_ref, rate_ref, out_ref, wide_ref, step_ref, rates_ref, pick_ref, ends_ref,
     state_ref, proj_ref, value_ref, sum_ref, back_ref) = refs[count:]
    positions, lines, share = out_ref.shape
    block = rows * lines
    me = me_ref[0]
    for shift in range(count):
        frm = lax.rem(me + count - shift, count)
        piece = got_refs[shift][:, :share].astype(F32).reshape(rows, lines, share)
        value_ref[pl.ds(frm * rows, rows)] = piece
        proj_ref[pl.ds(pl.multiple_of(frm * block, block), block), :] = got_refs[shift][:, share:]

        @pl.when(frm == 0)
        def _():
            value_ref[positions] = piece[0]
            proj_ref[pl.ds(positions * lines, lines), :] = got_refs[shift][:lines, share:]

    proj = proj_ref[lines:, :]
    prepare(proj, w_dt_ref, bias_ref, rate_ref, wide_ref, step_ref, rates_ref, pick_ref, ends_ref)
    values = value_ref.at[pl.ds(1, positions)]
    scan(step_ref, values, rates_ref, pick_ref, ends_ref, state_ref, sum_ref, back_ref)
    out_ref[...] = (sum_ref[...] + back_ref[...]).astype(BF16)


def vmem():
    return pl.BlockSpec(memory_space=pltpu.VMEM)


def smem():
    return pl.BlockSpec(memory_space=pltpu.SMEM)


def call(kernel, name, outs, scratch, *args, scalars=0, far=()):
    many = isinstance(outs, (list, tuple))
    hbm = pl.BlockSpec(memory_space=pltpu.HBM)
    return pl.pallas_call(
        kernel,
        name=name,
        out_shape=outs,
        in_specs=[smem()] * scalars + [vmem()] * (len(args) - scalars) + [hbm] * len(far),
        out_specs=[vmem()] * len(outs) if many else vmem(),
        scratch_shapes=scratch,
        compiler_params=pltpu.CompilerParams(vmem_limit_bytes=24 << 20),
    )(*args, *[pltpu.with_memory_space_constraint(x, pltpu.HBM) for x in far])


def array(shape, dtype=BF16):
    return pltpu.VMEM(shape, dtype)


def near(x):
    return pltpu.with_memory_space_constraint(x, pltpu.VMEM)


def like(x):
    return array(x.shape, x.dtype)


def scan_scratch(positions, lines, channels, width, state):
    return [
        pltpu.VMEM((width, 2 * channels), BF16),
        pltpu.VMEM((2, positions, lines, channels), F32),
        pltpu.VMEM((2, state, lines, channels), F32),
        pltpu.VMEM((state, 2 * state, 2 * LANES), BF16),
        pltpu.VMEM((2, positions * lines, 2 * state), BF16),
        pltpu.VMEM((2, state, lines, channels), F32),
    ]


def local(
    features, gate_branch, w_row_proj, w_dt_row, dt_bias_row, rate_row, skip_row,
    conv_taps, conv_bias, w_col_proj, w_dt_col, dt_bias_col, rate_col,
):
    rows, cols, channels = features.shape
    width = w_row_proj.shape[1]
    state = rate_row.shape[2]
    n_col, n_row = lax.axis_size("col"), lax.axis_size("row")
    share, col_share = channels // n_col, channels // n_row
    line, column = cols * n_col, rows * n_row
    tokens = rows * cols
    me = lax.axis_index("row").astype(jnp.int32).reshape(1)

    row_params = (w_dt_row, dt_bias_row, jnp.swapaxes(rate_row, 1, 2), skip_row.reshape(1, share))
    params = (
        conv_taps,
        conv_bias.reshape(1, share),
        w_col_proj,
        w_dt_col,
        dt_bias_col,
        jnp.swapaxes(rate_col, 1, 2),
    )
    sent, *row_params = call(
        pack_kernel,
        "pack",
        [array((n_col, tokens, 2 * share + width))] + [like(p) for p in row_params],
        [
            pltpu.VMEM(features.shape, BF16),
            pltpu.VMEM(gate_branch.shape, BF16),
            pltpu.VMEM(w_row_proj.shape, BF16),
            pltpu.SemaphoreType.DMA((3 + len(row_params),)),
        ],
        far=(features, gate_branch, w_row_proj, *row_params),
    )
    got = lax.all_to_all(sent, "col", 0, 0, tiled=True)
    got = near(got.reshape(line, rows, 2 * share + width))
    scratch = [
        pltpu.VMEM((line, rows, share), F32),
        pltpu.VMEM((line, rows, share), F32),
        pltpu.VMEM((line, rows, width), F32),
        pltpu.VMEM((line * rows, 2 * state), BF16),
        pltpu.VMEM((line, rows, share), F32),
    ]
    upper, tail, wide, rates, pick, *params = call(
        upper_kernel,
        "upper_rows",
        [
            array((line, rows, share)),
            array((2, line, share)),
            array((width, 2 * share)),
            array((state, rows, share), F32),
            array((state, 2 * state, 2 * LANES)),
        ]
        + [like(p) for p in params],
        scratch + [pltpu.SemaphoreType.DMA((len(params),))],
        got,
        *row_params,
        far=params,
    )
    above = lax.ppermute(tail, "row", [(i, (i + 1) % n_row) for i in range(n_row)])
    lower = call(
        functools.partial(lower_kernel, rank=w_dt_row.shape[1]),
        "lower_rows",
        array((line, rows, share)),
        scratch,
        got,
        row_params[1],
        row_params[3],
        near(wide),
        near(rates),
        near(pick),
    )
    sent = call(
        conv_kernel,
        "conv",
        array((n_col, tokens, share)),
        [pltpu.VMEM((line + 2, rows + 8, share), F32)],
        me,
        near(lower),
        near(upper),
        near(above),
        *params[:2],
        scalars=1,
    )
    got = lax.all_to_all(sent, "col", 0, 0, tiled=True)
    pieces = call(
        functools.partial(turn_kernel, rows=rows),
        "turn",
        [array((tokens, col_share + width))] * n_row,
        [],
        me,
        near(got),
        params[2],
        scalars=1,
    )
    pieces = [pieces[0]] + [
        lax.ppermute(pieces[s], "row", [(i, (i + s) % n_row) for i in range(n_row)]) for s in range(1, n_row)
    ]
    return call(
        functools.partial(col_kernel, count=n_row, rows=rows),
        "col_scan",
        jax.ShapeDtypeStruct((column, cols, col_share), BF16),
        scan_scratch(column, cols, col_share, width, state)
        + [
            pltpu.VMEM(((column + 1) * cols, width), BF16),
            pltpu.VMEM((column + 1, cols, col_share), F32),
            pltpu.VMEM((column, cols, col_share), F32),
            pltpu.VMEM((column, cols, col_share), F32),
        ],
        me,
        *[near(piece) for piece in pieces],
        *params[3:],
        scalars=1,
    )


def solution(mesh):
    return jax.shard_map(
        local,
        mesh=mesh,
        in_specs=(
            P("row", "col", None),
            P("row", "col", None),
            P(),
            P(None, None, "col"),
            P(None, "col"),
            P(None, "col", None),
            P("col"),
            P(None, None, "col"),
            P("col"),
            P(),
            P(None, None, "row"),
            P(None, "row"),
            P(None, "row", None),
        ),
        out_specs=P(None, "col", "row"),
        check_vma=False,
    )
```

```python
import functools
import math

import jax
import jax.numpy as jnp
from jax import lax
from jax.experimental import pallas as pl
from jax.experimental.pallas import tpu as pltpu
from jax.sharding import PartitionSpec as P

LANES = 128
F32 = jnp.float32
BF16 = jnp.bfloat16
LOG2E = math.log2(math.e)


def dot(a, b):
    return jnp.dot(a, b, preferred_element_type=F32)


def silu(v):
    return v / (1.0 + jnp.exp(-v))


def softplus(v):
    return jnp.maximum(v, 0.0) + jnp.log1p(jnp.exp(-jnp.abs(v)))


def shuffle(tokens, outer, inner):
    shape = (tokens, tokens)
    to = lax.broadcasted_iota(jnp.int32, shape, 0).astype(F32)
    frm = lax.broadcasted_iota(jnp.int32, shape, 1).astype(F32)
    high = jnp.floor((to + 0.5) / inner)
    wanted = jnp.where(to < outer * inner, (to - high * inner) * outer + high, to)
    return jnp.where(frm == wanted, 1.0, 0.0).astype(BF16)


def fetches(sources, targets, sems):
    copies = [pltpu.make_async_copy(s, t, sems.at[i]) for i, (s, t) in enumerate(zip(sources, targets))]
    for copy in copies:
        copy.start()
    return copies


def there(spot, shift):
    return spot // 2 ^ shift


def pack_kernel(spot_ref, feat_hbm, gate_hbm, w_hbm, *refs, chips):
    count = (len(refs) - 5 - chips) // 2
    param_refs, held_refs = refs[:count], refs[count + chips : 2 * count + chips]
    send_refs = refs[count : count + chips]
    feat_ref, gate_ref, w_ref, out_ref, sems = refs[2 * count + chips :]
    copies = fetches((feat_hbm, w_hbm, gate_hbm, *param_refs), (feat_ref, w_ref, gate_ref, *held_refs), sems)
    rows, cols, channels = feat_ref.shape
    tokens = rows * cols
    parts = out_ref.shape[0]
    share = channels // parts
    order = shuffle(tokens, cols, rows)
    copies[0].wait()
    feats = feat_ref[...].reshape(tokens, channels)
    moved = dot(order, feats).astype(BF16)
    for part in range(parts):
        out_ref[part, :, :share] = moved[:, part * share : (part + 1) * share]
    copies[1].wait()
    proj = dot(order, dot(feats, w_ref[...]).astype(BF16)).astype(BF16)
    for part in range(parts):
        out_ref[part, :, 2 * share :] = proj
    copies[2].wait()
    moved = dot(order, gate_ref[...].reshape(tokens, channels)).astype(BF16)
    for part in range(parts):
        out_ref[part, :, share : 2 * share] = moved[:, part * share : (part + 1) * share]
    spot = spot_ref[0]
    for shift in range(chips):
        for other in range(2):
            send_refs[shift][other] = out_ref[there(spot, shift) * 2 + (spot % 2 ^ other)]
    for copy in copies[3:]:
        copy.wait()


def gathered(spot, refs, put):
    chips = len(refs) // 2
    for shift in range(chips):
        for other in range(2):
            put(there(spot, shift) * 2 + (spot % 2 ^ other), refs[other * chips + shift][other])


def one_hot(height, width, hit):
    row = lax.broadcasted_iota(jnp.int32, (height, width), 0)
    column = lax.broadcasted_iota(jnp.int32, (height, width), 1)
    return jnp.where(hit(row, column), 1.0, 0.0).astype(BF16)


def prepare(proj, w_dt_ref, bias_ref, rate_ref, wide_ref, step_ref, rates_ref, pick_ref, ends_ref):
    _, rank, channels = w_dt_ref.shape
    state = rate_ref.shape[1]
    segment = rank + 2 * state
    lines = rates_ref.shape[2]
    wide_ref[...] = jnp.zeros_like(wide_ref)
    for k in range(2):
        wide_ref[pl.ds(k * segment, rank), pl.ds(k * channels, channels)] = w_dt_ref[k]
    raw = dot(proj, wide_ref[...])
    for k in range(2):
        part = raw[:, k * channels : (k + 1) * channels] + bias_ref[k : k + 1, :]
        step_ref[k] = softplus(part).reshape(step_ref.shape[1:])
        turned = rate_ref[k] * -LOG2E
        for n in range(state):
            rates_ref[k, n] = jnp.broadcast_to(turned[n : n + 1, :], (lines, channels))
        base = k * segment + rank
        ends_ref[k] = dot(proj, one_hot(proj.shape[1], 2 * state, lambda r, c: r == c + base)).astype(BF16)
    for n in range(state):
        pick_ref[n] = one_hot(2 * state, 2 * LANES, lambda r, c: r == n + jnp.where(c < LANES, 0, state))


def scan(step_ref, value_ref, rates_ref, pick_ref, ends_ref, state_ref, out_ref, back_ref):
    positions, lines, channels = out_ref.shape
    state = rates_ref.shape[1]
    width = min(channels, LANES)
    groups = [pl.ds(at, width) for at in range(0, channels, width)]
    size = math.gcd(positions, max(1, 32 // (lines * len(groups))))
    blocks = positions // size
    state_ref[...] = jnp.zeros_like(state_ref)

    def advance(at, _):
        firsts = (pl.multiple_of(at * size, size), pl.multiple_of((blocks - 1 - at) * size, size))
        orders = (list(range(size)), list(reversed(range(size))))
        steps, drives, ends = [], [], []
        for k, first in enumerate(firsts):
            steps.append([[step_ref[k, first + p, :, g] for g in groups] for p in range(size)])
            drives.append([[steps[k][p][i] * value_ref[first + p, :, g] for i, g in enumerate(groups)] for p in range(size)])
            ends.append(ends_ref[k, pl.ds(pl.multiple_of(first * lines, size * lines), size * lines), :])
        totals = [[[None] * len(groups) for _ in range(size)] for _ in firsts]
        both = jnp.concatenate(ends, axis=0)
        for n in range(state):
            spread = dot(both, pick_ref[n])
            held = [[state_ref[k, n, :, g] for g in groups] for k in range(2)]
            rates = [[rates_ref[k, n, :, g] for g in groups] for k in range(2)]
            for at_p in range(size):
                for k in range(2):
                    p = orders[k][at_p]
                    row = (k * size + p) * lines
                    b = spread[row : row + lines, :width]
                    c = spread[row : row + lines, LANES : LANES + width]
                    for i in range(len(groups)):
                        held[k][i] = jnp.exp2(steps[k][p][i] * rates[k][i]) * held[k][i] + drives[k][p][i] * b
                        read = c * held[k][i]
                        totals[k][p][i] = read if n == 0 else totals[k][p][i] + read
            for k in range(2):
                for i, g in enumerate(groups):
                    state_ref[k, n, :, g] = held[k][i]
        for p in range(size):
            for i, g in enumerate(groups):
                out_ref[firsts[0] + p, :, g] = totals[0][p][i]
                back_ref[firsts[1] + p, :, g] = totals[1][p][i]
        return 0

    lax.fori_loop(0, blocks, advance, 0, unroll=True)


def joint_scan(step_ref, value_ref, rates_ref, pick_ref, ends_ref, out_ref):
    positions, lines, channels = out_ref.shape
    state = rates_ref.shape[0]
    size = math.gcd(positions, 8)
    held = [jnp.zeros((lines, channels), F32)] * state
    for first in range(0, positions, size):
        steps = [step_ref[first + p] for p in range(size)]
        drives = [steps[p] * value_ref[first + p] for p in range(size)]
        totals = [None] * size
        ends = ends_ref[first * lines : (first + size) * lines, :]
        for n in range(state):
            spread = dot(ends, pick_ref[n])
            rates = rates_ref[n]
            for p in range(size):
                b = spread[p * lines : (p + 1) * lines, :channels]
                c = spread[p * lines : (p + 1) * lines, LANES : LANES + channels]
                held[n] = jnp.exp2(steps[p] * rates) * held[n] + drives[p] * b
                read = c * held[n]
                totals[p] = read if n == 0 else totals[p] + read
        for p in range(size):
            out_ref[first + p] = totals[p]


def row_tables(w_dt_ref, rate_ref, wide_ref, rates_ref, pick_ref):
    _, rank, channels = w_dt_ref.shape
    state = rate_ref.shape[1]
    segment = rank + 2 * state
    lines = rates_ref.shape[1]
    low = lax.broadcasted_iota(jnp.int32, (lines, channels), 0) < lines // 2
    wide_ref[...] = jnp.zeros_like(wide_ref)
    for k in range(2):
        wide_ref[pl.ds(k * segment, rank), pl.ds(k * channels, channels)] = w_dt_ref[k]
    turned = [rate_ref[k] * -LOG2E for k in range(2)]
    for n in range(state):
        rates_ref[n] = jnp.where(low, *[jnp.broadcast_to(t[n : n + 1, :], (lines, channels)) for t in turned])
        pick_ref[n] = one_hot(2 * state, 2 * LANES, lambda r, c: r == n + jnp.where(c < LANES, 0, state))


def half_rows(upper, rank, got_ref, bias_ref, skip_ref, wide_ref, rates_ref, pick_ref, out_ref, scratch):
    step_ref, value_ref, proj_ref, ends_ref, sum_ref = scratch
    positions, lines, share = out_ref.shape
    state = rates_ref.shape[0]
    segment = rank + 2 * state
    width = proj_ref.shape[2]
    half = lines // 2

    def low(columns):
        return lax.broadcasted_iota(jnp.int32, (lines, columns), 0) < half

    def swap(v):
        return pltpu.roll(v, half, 0)

    def packed(p, at):
        there = got_ref[p, :, at].astype(F32)
        back = got_ref[positions - 1 - p, :, at].astype(F32)
        there, back = (swap(there), back) if upper else (there, swap(back))
        return jnp.where(low(there.shape[1]), there, back)

    for p in range(positions):
        value_ref[p] = packed(p, pl.ds(0, share))
        proj_ref[p] = packed(p, pl.ds(2 * share, width))
    proj = proj_ref[...].reshape(positions * lines, width).astype(BF16)
    raw = dot(proj, wide_ref[...])
    parts = [(raw[:, k * share : (k + 1) * share] + bias_ref[k : k + 1, :]).reshape(positions, lines, share) for k in range(2)]
    step_ref[...] = softplus(jnp.where(low(share), *parts))
    ends = [
        dot(proj, one_hot(width, 2 * state, lambda r, c: r == c + k * segment + rank)).reshape(positions, lines, 2 * state)
        for k in range(2)
    ]
    ends_ref[...] = jnp.where(low(2 * state), *ends).reshape(ends_ref.shape).astype(BF16)
    joint_scan(step_ref, value_ref, rates_ref, pick_ref, ends_ref, sum_ref)
    for p in range(positions):
        there, back = sum_ref[p], sum_ref[positions - 1 - p]
        mix = swap(there) + back if upper else there + swap(back)
        mix = mix + skip_ref[...] * got_ref[p, :, :share].astype(F32)
        gated = mix * silu(got_ref[p, :, share : 2 * share].astype(F32))
        value_ref[p] = gated
        out_ref[p] = gated.astype(BF16)


def upper_kernel(spot_ref, *refs, sources):
    block_refs, (w_dt_ref, bias_ref, rate_ref, skip_ref), refs = refs[:sources], refs[sources : sources + 4], refs[sources + 4 :]
    out_ref, tail_ref, wide_ref, rates_ref, pick_ref, got_ref, *scratch = refs
    positions, lines, share = out_ref.shape
    cols = positions // sources

    def put(place, block):
        got_ref[pl.ds(place * cols, cols)] = block.reshape(cols, lines, block.shape[1])

    gathered(spot_ref[0], block_refs, put)
    row_tables(w_dt_ref, rate_ref, wide_ref, rates_ref, pick_ref)
    half_rows(True, w_dt_ref.shape[1], got_ref, bias_ref, skip_ref, wide_ref, rates_ref, pick_ref, out_ref, scratch)
    flat_ref = scratch[1].reshape(positions * lines, share)
    for j in range(2):
        tail_ref[j] = flat_ref[pl.ds(lines - 2 + j, positions, stride=lines), :].astype(BF16)


def lower_kernel(got_ref, bias_ref, skip_ref, wide_ref, rates_ref, pick_ref, *refs, rank):
    *scratch, sems = refs[-6:]
    count = (len(refs) - 7) // 2
    out_ref, *held_refs = refs[count:-6]
    copies = fetches(refs[:count], held_refs, sems)
    half_rows(False, rank, got_ref, bias_ref, skip_ref, wide_ref, rates_ref, pick_ref, out_ref, scratch)
    for copy in copies:
        copy.wait()


def conv_kernel(me_ref, spot_ref, lower_ref, upper_ref, above_ref, taps_ref, bias_ref, *refs):
    *send_refs, pad_ref = refs
    positions, lines, share = lower_ref.shape
    cols = positions // (2 * len(send_refs))
    height = pad_ref.shape[1]
    top = height - lines
    zero_edge = jnp.zeros((1, height, share), F32)
    pad_ref[0:1] = zero_edge
    pad_ref[positions + 1 : positions + 2] = zero_edge
    slot = lax.broadcasted_iota(jnp.int32, (lines, share), 0)
    mid = jnp.where(slot < lines // 2, lower_ref[...].astype(F32), upper_ref[...].astype(F32))
    pad_ref[1 : positions + 1, top:, :] = mid
    flat_ref = pad_ref.reshape((positions + 2) * height, share)
    for j in range(2):
        flat_ref[pl.ds(height + top - 2 + j, positions, stride=height), :] = above_ref[j].astype(F32)
    first = me_ref[0] == 0
    beyond = (jnp.logical_and(first, slot == 1), None, jnp.logical_and(first, slot == 0))
    taps = []
    for i in range(3):
        wide = [jnp.broadcast_to(taps_ref[i, j : j + 1, :], (lines, share)) for j in range(3)]
        taps.append(wide if beyond[i] is None else [jnp.where(beyond[i], 0.0, tap) for tap in wide])
    bias = jnp.broadcast_to(bias_ref[...], (lines, share))

    spot = spot_ref[0]
    for shift, send_ref in enumerate(send_refs):
        for other in range(2):
            start = (there(spot, shift) * 2 + (spot % 2 ^ other)) * cols
            for w in range(cols):
                total = bias
                for i in range(3):
                    for j in range(3):
                        total = total + taps[i][j] * pad_ref[start + w + j, top - 2 + i : top - 2 + i + lines, :]
                send_ref[other, w * lines : (w + 1) * lines, :] = silu(total).astype(BF16)


def turn_kernel(me_ref, spot_ref, *refs, sources, rows):
    block_refs, w_ref, out_refs, got_ref = refs[:sources], refs[sources], refs[sources + 1 : -1], refs[-1]
    parts, tokens, share = got_ref.shape
    width = w_ref.shape[1]
    count = len(out_refs)
    each = parts // count
    order = shuffle(tokens, rows, tokens // rows)
    sums = []

    def put(place, block):
        got_ref[place] = block
        sums.append(dot(block, w_ref[pl.ds(pl.multiple_of(place * share, share), share), :]))

    gathered(spot_ref[0], block_refs, put)
    proj = dot(order, sum(sums).astype(BF16)).astype(BF16)
    me = me_ref[0]
    for shift in range(count):
        to = lax.rem(me + shift, count)
        for j in range(each):
            moved = dot(order, got_ref[to * each + j]).astype(BF16)
            out_refs[shift][:, j * share : (j + 1) * share] = moved
        out_refs[shift][:, each * share :] = proj


def col_kernel(
    me_ref, *refs, count, rows,
):
    got_refs = refs[:count]
    (w_dt_ref, bias_ref, rate_ref, out_ref, wide_ref, step_ref, rates_ref, pick_ref, ends_ref,
     state_ref, proj_ref, value_ref, sum_ref, back_ref) = refs[count:]
    positions, lines, share = out_ref.shape
    block = rows * lines
    me = me_ref[0]
    for shift in range(count):
        frm = lax.rem(me + count - shift, count)
        piece = got_refs[shift][:, :share].astype(F32).reshape(rows, lines, share)
        value_ref[pl.ds(frm * rows, rows)] = piece
        proj_ref[pl.ds(pl.multiple_of(frm * block, block), block), :] = got_refs[shift][:, share:]

        @pl.when(frm == 0)
        def _():
            value_ref[positions] = piece[0]
            proj_ref[pl.ds(positions * lines, lines), :] = got_refs[shift][:lines, share:]

    proj = proj_ref[lines:, :]
    prepare(proj, w_dt_ref, bias_ref, rate_ref, wide_ref, step_ref, rates_ref, pick_ref, ends_ref)
    values = value_ref.at[pl.ds(1, positions)]
    scan(step_ref, values, rates_ref, pick_ref, ends_ref, state_ref, sum_ref, back_ref)
    out_ref[...] = (sum_ref[...] + back_ref[...]).astype(BF16)


def vmem():
    return pl.BlockSpec(memory_space=pltpu.VMEM)


def smem():
    return pl.BlockSpec(memory_space=pltpu.SMEM)


def call(kernel, name, outs, scratch, *args, scalars=0, far=()):
    many = isinstance(outs, (list, tuple))
    hbm = pl.BlockSpec(memory_space=pltpu.HBM)
    return pl.pallas_call(
        kernel,
        name=name,
        out_shape=outs,
        in_specs=[smem()] * scalars + [vmem()] * (len(args) - scalars) + [hbm] * len(far),
        out_specs=[vmem()] * len(outs) if many else vmem(),
        scratch_shapes=scratch,
        compiler_params=pltpu.CompilerParams(vmem_limit_bytes=24 << 20),
    )(*args, *[pltpu.with_memory_space_constraint(x, pltpu.HBM) for x in far])


def array(shape, dtype=BF16):
    return pltpu.VMEM(shape, dtype)


def near(x):
    return pltpu.with_memory_space_constraint(x, pltpu.VMEM)


def like(x):
    return array(x.shape, x.dtype)


def scan_scratch(positions, lines, channels, width, state):
    return [
        pltpu.VMEM((width, 2 * channels), BF16),
        pltpu.VMEM((2, positions, lines, channels), F32),
        pltpu.VMEM((2, state, lines, channels), F32),
        pltpu.VMEM((state, 2 * state, 2 * LANES), BF16),
        pltpu.VMEM((2, positions * lines, 2 * state), BF16),
        pltpu.VMEM((2, state, lines, channels), F32),
    ]


def local(
    features, gate_branch, w_row_proj, w_dt_row, dt_bias_row, rate_row, skip_row,
    conv_taps, conv_bias, w_col_proj, w_dt_col, dt_bias_col, rate_col,
):
    rows, cols, channels = features.shape
    width = w_row_proj.shape[1]
    state = rate_row.shape[2]
    n_col, n_row = lax.axis_size("col"), lax.axis_size("row")
    share, col_share = channels // n_col, channels // n_row
    line, column = cols * n_col, rows * n_row
    tokens = rows * cols
    me = lax.axis_index("row").astype(jnp.int32).reshape(1)
    spot = lax.axis_index("col").astype(jnp.int32).reshape(1)
    chips = n_col // 2

    def exchange(pieces):
        pieces = [pieces[0]] + [
            lax.ppermute(pieces[s], "col", [(i, (i // 2 ^ s) * 2 + i % 2) for i in range(n_col)]) for s in range(1, chips)
        ]
        passed = [lax.ppermute(piece, "col", [(i, i ^ 1) for i in range(n_col)]) for piece in pieces]
        return [near(piece) for piece in pieces + passed]


    row_params = (w_dt_row, dt_bias_row, jnp.swapaxes(rate_row, 1, 2), skip_row.reshape(1, share))
    params = (
        conv_taps,
        conv_bias.reshape(1, share),
        w_col_proj,
        w_dt_col,
        dt_bias_col,
        jnp.swapaxes(rate_col, 1, 2),
    )
    sent = call(
        functools.partial(pack_kernel, chips=chips),
        "pack",
        [array((2, tokens, 2 * share + width))] * chips + [like(p) for p in row_params],
        [
            pltpu.VMEM(features.shape, BF16),
            pltpu.VMEM(gate_branch.shape, BF16),
            pltpu.VMEM(w_row_proj.shape, BF16),
            pltpu.VMEM((n_col, tokens, 2 * share + width), BF16),
            pltpu.SemaphoreType.DMA((3 + len(row_params),)),
        ],
        spot,
        scalars=1,
        far=(features, gate_branch, w_row_proj, *row_params),
    )
    sent, row_params = sent[:chips], sent[chips:]
    blocks = exchange(sent)
    scratch = [
        pltpu.VMEM((line, rows, share), F32),
        pltpu.VMEM((line, rows, share), F32),
        pltpu.VMEM((line, rows, width), F32),
        pltpu.VMEM((line * rows, 2 * state), BF16),
        pltpu.VMEM((line, rows, share), F32),
    ]
    upper, tail, wide, rates, pick, got = call(
        functools.partial(upper_kernel, sources=n_col),
        "upper_rows",
        [
            array((line, rows, share)),
            array((2, line, share)),
            array((width, 2 * share)),
            array((state, rows, share), F32),
            array((state, 2 * state, 2 * LANES)),
            array((line, rows, 2 * share + width)),
        ],
        scratch,
        spot,
        *blocks,
        *row_params,
        scalars=1,
    )
    above = lax.ppermute(tail, "row", [(i, (i + 1) % n_row) for i in range(n_row)])
    lower, *params = call(
        functools.partial(lower_kernel, rank=w_dt_row.shape[1]),
        "lower_rows",
        [array((line, rows, share))] + [like(p) for p in params],
        scratch + [pltpu.SemaphoreType.DMA((len(params),))],
        near(got),
        row_params[1],
        row_params[3],
        near(wide),
        near(rates),
        near(pick),
        far=params,
    )
    sent = call(
        conv_kernel,
        "conv",
        [array((2, tokens, share))] * chips,
        [pltpu.VMEM((line + 2, rows + 8, share), F32)],
        me,
        spot,
        near(lower),
        near(upper),
        near(above),
        *params[:2],
        scalars=2,
    )
    blocks = exchange(sent)
    pieces = call(
        functools.partial(turn_kernel, sources=n_col, rows=rows),
        "turn",
        [array((tokens, col_share + width))] * n_row,
        [pltpu.VMEM((n_col, tokens, share), BF16)],
        me,
        spot,
        *blocks,
        params[2],
        scalars=2,
    )
    pieces = [pieces[0]] + [
        lax.ppermute(pieces[s], "row", [(i, (i + s) % n_row) for i in range(n_row)]) for s in range(1, n_row)
    ]
    return call(
        functools.partial(col_kernel, count=n_row, rows=rows),
        "col_scan",
        jax.ShapeDtypeStruct((column, cols, col_share), BF16),
        scan_scratch(column, cols, col_share, width, state)
        + [
            pltpu.VMEM(((column + 1) * cols, width), BF16),
            pltpu.VMEM((column + 1, cols, col_share), F32),
            pltpu.VMEM((column, cols, col_share), F32),
            pltpu.VMEM((column, cols, col_share), F32),
        ],
        me,
        *[near(piece) for piece in pieces],
        *params[3:],
        scalars=1,
    )


def solution(mesh):
    return jax.shard_map(
        local,
        mesh=mesh,
        in_specs=(
            P("row", "col", None),
            P("row", "col", None),
            P(),
            P(None, None, "col"),
            P(None, "col"),
            P(None, "col", None),
            P("col"),
            P(None, None, "col"),
            P("col"),
            P(),
            P(None, None, "row"),
            P(None, "row"),
            P(None, "row", None),
        ),
        out_specs=P(None, "col", "row"),
        check_vma=False,
    )
```

```python
import functools
import math

import jax
import jax.numpy as jnp
from jax import lax
from jax.experimental import pallas as pl
from jax.experimental.pallas import tpu as pltpu
from jax.sharding import PartitionSpec as P

LANES = 128
F32 = jnp.float32
BF16 = jnp.bfloat16
LOG2E = math.log2(math.e)


def dot(a, b):
    return jnp.dot(a, b, preferred_element_type=F32)


def silu(v):
    return v / (1.0 + jnp.exp(-v))


def softplus(v):
    return jnp.maximum(v, 0.0) + jnp.log1p(jnp.exp(-jnp.abs(v)))


def shuffle(tokens, outer, inner):
    shape = (tokens, tokens)
    to = lax.broadcasted_iota(jnp.int32, shape, 0).astype(F32)
    frm = lax.broadcasted_iota(jnp.int32, shape, 1).astype(F32)
    high = jnp.floor((to + 0.5) / inner)
    wanted = jnp.where(to < outer * inner, (to - high * inner) * outer + high, to)
    return jnp.where(frm == wanted, 1.0, 0.0).astype(BF16)


def fetches(sources, targets, sems):
    copies = [pltpu.make_async_copy(s, t, sems.at[i]) for i, (s, t) in enumerate(zip(sources, targets))]
    for copy in copies:
        copy.start()
    return copies


def shifts(chips):
    return [0, *([chips - 1] if chips > 1 else []), *range(1, chips - 1)]


def there(spot, shift):
    return spot // 2 ^ shift


def place(spot, shift, other):
    return there(spot, shift) * 2 + (spot % 2 ^ other)


def pack_kernel(spot_ref, feat_hbm, gate_hbm, w_hbm, *refs, chips):
    count = (len(refs) - 5 - chips) // 2
    param_refs, held_refs = refs[:count], refs[count + chips : 2 * count + chips]
    send_refs = refs[count : count + chips]
    feat_ref, gate_ref, w_ref, out_ref, sems = refs[2 * count + chips :]
    copies = fetches((feat_hbm, w_hbm, gate_hbm, *param_refs), (feat_ref, w_ref, gate_ref, *held_refs), sems)
    rows, cols, channels = feat_ref.shape
    tokens = rows * cols
    parts = out_ref.shape[0]
    share = channels // parts
    order = shuffle(tokens, cols, rows)
    copies[0].wait()
    feats = feat_ref[...].reshape(tokens, channels)
    moved = dot(order, feats).astype(BF16)
    for part in range(parts):
        out_ref[part, :, :share] = moved[:, part * share : (part + 1) * share]
    copies[1].wait()
    proj = dot(order, dot(feats, w_ref[...]).astype(BF16)).astype(BF16)
    for part in range(parts):
        out_ref[part, :, 2 * share :] = proj
    copies[2].wait()
    moved = dot(order, gate_ref[...].reshape(tokens, channels)).astype(BF16)
    for part in range(parts):
        out_ref[part, :, share : 2 * share] = moved[:, part * share : (part + 1) * share]
    for shift, send_ref in zip(shifts(chips), send_refs):
        for other in range(2):
            send_ref[other] = out_ref[place(spot_ref[0], shift, other)]
    for copy in copies[3:]:
        copy.wait()


def gathered(spot, refs, put):
    chips = len(refs) // 2
    for at, shift in enumerate(shifts(chips)):
        for other in range(2):
            put(place(spot, shift, other), refs[other * chips + at][other])


def one_hot(height, width, hit):
    row = lax.broadcasted_iota(jnp.int32, (height, width), 0)
    column = lax.broadcasted_iota(jnp.int32, (height, width), 1)
    return jnp.where(hit(row, column), 1.0, 0.0).astype(BF16)


def prepare(proj, w_dt_ref, bias_ref, rate_ref, wide_ref, step_ref, rates_ref, pick_ref, ends_ref):
    _, rank, channels = w_dt_ref.shape
    state = rate_ref.shape[1]
    segment = rank + 2 * state
    lines = rates_ref.shape[2]
    wide_ref[...] = jnp.zeros_like(wide_ref)
    for k in range(2):
        wide_ref[pl.ds(k * segment, rank), pl.ds(k * channels, channels)] = w_dt_ref[k]
    raw = dot(proj, wide_ref[...])
    for k in range(2):
        part = raw[:, k * channels : (k + 1) * channels] + bias_ref[k : k + 1, :]
        step_ref[k] = softplus(part).reshape(step_ref.shape[1:])
        turned = rate_ref[k] * -LOG2E
        for n in range(state):
            rates_ref[k, n] = jnp.broadcast_to(turned[n : n + 1, :], (lines, channels))
        base = k * segment + rank
        ends_ref[k] = dot(proj, one_hot(proj.shape[1], 2 * state, lambda r, c: r == c + base)).astype(BF16)
    for n in range(state):
        pick_ref[n] = one_hot(2 * state, 2 * LANES, lambda r, c: r == n + jnp.where(c < LANES, 0, state))


def scan(step_ref, value_ref, rates_ref, pick_ref, ends_ref, state_ref, out_ref, back_ref):
    positions, lines, channels = out_ref.shape
    state = rates_ref.shape[1]
    width = min(channels, LANES)
    groups = [pl.ds(at, width) for at in range(0, channels, width)]
    size = math.gcd(positions, max(1, 32 // (lines * len(groups))))
    blocks = positions // size
    state_ref[...] = jnp.zeros_like(state_ref)

    def advance(at, _):
        firsts = (pl.multiple_of(at * size, size), pl.multiple_of((blocks - 1 - at) * size, size))
        orders = (list(range(size)), list(reversed(range(size))))
        steps, drives, ends = [], [], []
        for k, first in enumerate(firsts):
            steps.append([[step_ref[k, first + p, :, g] for g in groups] for p in range(size)])
            drives.append([[steps[k][p][i] * value_ref[first + p, :, g] for i, g in enumerate(groups)] for p in range(size)])
            ends.append(ends_ref[k, pl.ds(pl.multiple_of(first * lines, size * lines), size * lines), :])
        totals = [[[None] * len(groups) for _ in range(size)] for _ in firsts]
        both = jnp.concatenate(ends, axis=0)
        for n in range(state):
            spread = dot(both, pick_ref[n])
            held = [[state_ref[k, n, :, g] for g in groups] for k in range(2)]
            rates = [[rates_ref[k, n, :, g] for g in groups] for k in range(2)]
            for at_p in range(size):
                for k in range(2):
                    p = orders[k][at_p]
                    row = (k * size + p) * lines
                    b = spread[row : row + lines, :width]
                    c = spread[row : row + lines, LANES : LANES + width]
                    for i in range(len(groups)):
                        held[k][i] = jnp.exp2(steps[k][p][i] * rates[k][i]) * held[k][i] + drives[k][p][i] * b
                        read = c * held[k][i]
                        totals[k][p][i] = read if n == 0 else totals[k][p][i] + read
            for k in range(2):
                for i, g in enumerate(groups):
                    state_ref[k, n, :, g] = held[k][i]
        for p in range(size):
            for i, g in enumerate(groups):
                out_ref[firsts[0] + p, :, g] = totals[0][p][i]
                back_ref[firsts[1] + p, :, g] = totals[1][p][i]
        return 0

    lax.fori_loop(0, blocks, advance, 0, unroll=True)


def joint_scan(step_ref, value_ref, rates_ref, pick_ref, ends_ref, out_ref):
    positions, lines, channels = out_ref.shape
    state = rates_ref.shape[0]
    size = math.gcd(positions, 8)
    held = [jnp.zeros((lines, channels), F32)] * state
    for first in range(0, positions, size):
        steps = [step_ref[first + p] for p in range(size)]
        drives = [steps[p] * value_ref[first + p] for p in range(size)]
        totals = [None] * size
        ends = ends_ref[first * lines : (first + size) * lines, :]
        for n in range(state):
            spread = dot(ends, pick_ref[n])
            rates = rates_ref[n]
            for p in range(size):
                b = spread[p * lines : (p + 1) * lines, :channels]
                c = spread[p * lines : (p + 1) * lines, LANES : LANES + channels]
                held[n] = jnp.exp2(steps[p] * rates) * held[n] + drives[p] * b
                read = c * held[n]
                totals[p] = read if n == 0 else totals[p] + read
        for p in range(size):
            out_ref[first + p] = totals[p]


def row_tables(w_dt_ref, rate_ref, wide_ref, rates_ref, pick_ref):
    _, rank, channels = w_dt_ref.shape
    state = rate_ref.shape[1]
    segment = rank + 2 * state
    lines = rates_ref.shape[1]
    low = lax.broadcasted_iota(jnp.int32, (lines, channels), 0) < lines // 2
    wide_ref[...] = jnp.zeros_like(wide_ref)
    for k in range(2):
        wide_ref[pl.ds(k * segment, rank), pl.ds(k * channels, channels)] = w_dt_ref[k]
    turned = [rate_ref[k] * -LOG2E for k in range(2)]
    for n in range(state):
        rates_ref[n] = jnp.where(low, *[jnp.broadcast_to(t[n : n + 1, :], (lines, channels)) for t in turned])
        pick_ref[n] = one_hot(2 * state, 2 * LANES, lambda r, c: r == n + jnp.where(c < LANES, 0, state))


def half_rows(upper, rank, got_ref, bias_ref, skip_ref, wide_ref, rates_ref, pick_ref, out_ref, scratch):
    step_ref, value_ref, proj_ref, ends_ref, sum_ref = scratch
    positions, lines, share = out_ref.shape
    state = rates_ref.shape[0]
    segment = rank + 2 * state
    width = proj_ref.shape[2]
    half = lines // 2

    def low(columns):
        return lax.broadcasted_iota(jnp.int32, (lines, columns), 0) < half

    def swap(v):
        return pltpu.roll(v, half, 0)

    def packed(p, at):
        there = got_ref[p, :, at].astype(F32)
        back = got_ref[positions - 1 - p, :, at].astype(F32)
        there, back = (swap(there), back) if upper else (there, swap(back))
        return jnp.where(low(there.shape[1]), there, back)

    for p in range(positions):
        value_ref[p] = packed(p, pl.ds(0, share))
        proj_ref[p] = packed(p, pl.ds(2 * share, width))
    proj = proj_ref[...].reshape(positions * lines, width).astype(BF16)
    raw = dot(proj, wide_ref[...])
    parts = [(raw[:, k * share : (k + 1) * share] + bias_ref[k : k + 1, :]).reshape(positions, lines, share) for k in range(2)]
    step_ref[...] = softplus(jnp.where(low(share), *parts))
    ends = [
        dot(proj, one_hot(width, 2 * state, lambda r, c: r == c + k * segment + rank)).reshape(positions, lines, 2 * state)
        for k in range(2)
    ]
    ends_ref[...] = jnp.where(low(2 * state), *ends).reshape(ends_ref.shape).astype(BF16)
    joint_scan(step_ref, value_ref, rates_ref, pick_ref, ends_ref, sum_ref)
    for p in range(positions):
        there, back = sum_ref[p], sum_ref[positions - 1 - p]
        mix = swap(there) + back if upper else there + swap(back)
        mix = mix + skip_ref[...] * got_ref[p, :, :share].astype(F32)
        gated = mix * silu(got_ref[p, :, share : 2 * share].astype(F32))
        value_ref[p] = gated
        out_ref[p] = gated.astype(BF16)


def upper_kernel(spot_ref, *refs, sources):
    block_refs, (w_dt_ref, bias_ref, rate_ref, skip_ref), refs = refs[:sources], refs[sources : sources + 4], refs[sources + 4 :]
    out_ref, tail_ref, wide_ref, rates_ref, pick_ref, got_ref, *scratch = refs
    positions, lines, share = out_ref.shape
    cols = positions // sources

    def put(source, block):
        got_ref[pl.ds(source * cols, cols)] = block.reshape(cols, lines, block.shape[1])

    gathered(spot_ref[0], block_refs, put)
    row_tables(w_dt_ref, rate_ref, wide_ref, rates_ref, pick_ref)
    half_rows(True, w_dt_ref.shape[1], got_ref, bias_ref, skip_ref, wide_ref, rates_ref, pick_ref, out_ref, scratch)
    flat_ref = scratch[1].reshape(positions * lines, share)
    for j in range(2):
        tail_ref[j] = flat_ref[pl.ds(lines - 2 + j, positions, stride=lines), :].astype(BF16)


def lower_kernel(got_ref, bias_ref, skip_ref, wide_ref, rates_ref, pick_ref, *refs, rank):
    *scratch, sems = refs[-6:]
    count = (len(refs) - 7) // 2
    out_ref, *held_refs = refs[count:-6]
    copies = fetches(refs[:count], held_refs, sems)
    half_rows(False, rank, got_ref, bias_ref, skip_ref, wide_ref, rates_ref, pick_ref, out_ref, scratch)
    for copy in copies:
        copy.wait()


def conv_kernel(me_ref, spot_ref, lower_ref, upper_ref, above_ref, taps_ref, bias_ref, *refs):
    *send_refs, pad_ref = refs
    positions, lines, share = lower_ref.shape
    cols = positions // (2 * len(send_refs))
    height = pad_ref.shape[1]
    top = height - lines
    zero_edge = jnp.zeros((1, height, share), F32)
    pad_ref[0:1] = zero_edge
    pad_ref[positions + 1 : positions + 2] = zero_edge
    slot = lax.broadcasted_iota(jnp.int32, (lines, share), 0)
    mid = jnp.where(slot < lines // 2, lower_ref[...].astype(F32), upper_ref[...].astype(F32))
    pad_ref[1 : positions + 1, top:, :] = mid
    flat_ref = pad_ref.reshape((positions + 2) * height, share)
    for j in range(2):
        flat_ref[pl.ds(height + top - 2 + j, positions, stride=height), :] = above_ref[j].astype(F32)
    first = me_ref[0] == 0
    beyond = (jnp.logical_and(first, slot == 1), None, jnp.logical_and(first, slot == 0))
    taps = []
    for i in range(3):
        wide = [jnp.broadcast_to(taps_ref[i, j : j + 1, :], (lines, share)) for j in range(3)]
        taps.append(wide if beyond[i] is None else [jnp.where(beyond[i], 0.0, tap) for tap in wide])
    bias = jnp.broadcast_to(bias_ref[...], (lines, share))

    spot = spot_ref[0]
    for shift, send_ref in zip(shifts(len(send_refs)), send_refs):
        for other in range(2):
            start = place(spot, shift, other) * cols
            for w in range(cols):
                total = bias
                for i in range(3):
                    for j in range(3):
                        total = total + taps[i][j] * pad_ref[start + w + j, top - 2 + i : top - 2 + i + lines, :]
                send_ref[other, w * lines : (w + 1) * lines, :] = silu(total).astype(BF16)


def turn_kernel(me_ref, spot_ref, *refs, sources, rows):
    block_refs, w_ref, out_refs, got_ref = refs[:sources], refs[sources], refs[sources + 1 : -1], refs[-1]
    parts, tokens, share = got_ref.shape
    width = w_ref.shape[1]
    count = len(out_refs)
    each = parts // count
    order = shuffle(tokens, rows, tokens // rows)
    sums = []

    def put(source, block):
        got_ref[source] = block
        sums.append(dot(block, w_ref[pl.ds(pl.multiple_of(source * share, share), share), :]))

    gathered(spot_ref[0], block_refs, put)
    proj = dot(order, sum(sums).astype(BF16)).astype(BF16)
    me = me_ref[0]
    for shift in range(count):
        to = lax.rem(me + shift, count)
        for j in range(each):
            moved = dot(order, got_ref[to * each + j]).astype(BF16)
            out_refs[shift][:, j * share : (j + 1) * share] = moved
        out_refs[shift][:, each * share :] = proj


def col_kernel(
    me_ref, *refs, count, rows,
):
    got_refs = refs[:count]
    (w_dt_ref, bias_ref, rate_ref, out_ref, wide_ref, step_ref, rates_ref, pick_ref, ends_ref,
     state_ref, proj_ref, value_ref, sum_ref, back_ref) = refs[count:]
    positions, lines, share = out_ref.shape
    block = rows * lines
    me = me_ref[0]
    for shift in range(count):
        frm = lax.rem(me + count - shift, count)
        piece = got_refs[shift][:, :share].astype(F32).reshape(rows, lines, share)
        value_ref[pl.ds(frm * rows, rows)] = piece
        proj_ref[pl.ds(pl.multiple_of(frm * block, block), block), :] = got_refs[shift][:, share:]

        @pl.when(frm == 0)
        def _():
            value_ref[positions] = piece[0]
            proj_ref[pl.ds(positions * lines, lines), :] = got_refs[shift][:lines, share:]

    proj = proj_ref[lines:, :]
    prepare(proj, w_dt_ref, bias_ref, rate_ref, wide_ref, step_ref, rates_ref, pick_ref, ends_ref)
    values = value_ref.at[pl.ds(1, positions)]
    scan(step_ref, values, rates_ref, pick_ref, ends_ref, state_ref, sum_ref, back_ref)
    out_ref[...] = (sum_ref[...] + back_ref[...]).astype(BF16)


def vmem():
    return pl.BlockSpec(memory_space=pltpu.VMEM)


def smem():
    return pl.BlockSpec(memory_space=pltpu.SMEM)


def call(kernel, name, outs, scratch, *args, scalars=0, far=()):
    many = isinstance(outs, (list, tuple))
    hbm = pl.BlockSpec(memory_space=pltpu.HBM)
    return pl.pallas_call(
        kernel,
        name=name,
        out_shape=outs,
        in_specs=[smem()] * scalars + [vmem()] * (len(args) - scalars) + [hbm] * len(far),
        out_specs=[vmem()] * len(outs) if many else vmem(),
        scratch_shapes=scratch,
        compiler_params=pltpu.CompilerParams(vmem_limit_bytes=24 << 20),
    )(*args, *[pltpu.with_memory_space_constraint(x, pltpu.HBM) for x in far])


def array(shape, dtype=BF16):
    return pltpu.VMEM(shape, dtype)


def near(x):
    return pltpu.with_memory_space_constraint(x, pltpu.VMEM)


def like(x):
    return array(x.shape, x.dtype)


def scan_scratch(positions, lines, channels, width, state):
    return [
        pltpu.VMEM((width, 2 * channels), BF16),
        pltpu.VMEM((2, positions, lines, channels), F32),
        pltpu.VMEM((2, state, lines, channels), F32),
        pltpu.VMEM((state, 2 * state, 2 * LANES), BF16),
        pltpu.VMEM((2, positions * lines, 2 * state), BF16),
        pltpu.VMEM((2, state, lines, channels), F32),
    ]


def local(
    features, gate_branch, w_row_proj, w_dt_row, dt_bias_row, rate_row, skip_row,
    conv_taps, conv_bias, w_col_proj, w_dt_col, dt_bias_col, rate_col,
):
    rows, cols, channels = features.shape
    width = w_row_proj.shape[1]
    state = rate_row.shape[2]
    n_col, n_row = lax.axis_size("col"), lax.axis_size("row")
    share, col_share = channels // n_col, channels // n_row
    line, column = cols * n_col, rows * n_row
    tokens = rows * cols
    me = lax.axis_index("row").astype(jnp.int32).reshape(1)
    spot = lax.axis_index("col").astype(jnp.int32).reshape(1)
    chips = n_col // 2

    def exchange(pieces):
        pieces = [pieces[0]] + [
            lax.ppermute(piece, "col", [(i, place(i, s, 0)) for i in range(n_col)])
            for s, piece in list(zip(shifts(chips), pieces))[1:]
        ]
        passed = [lax.ppermute(piece, "col", [(i, i ^ 1) for i in range(n_col)]) for piece in pieces]
        return [near(piece) for piece in pieces + passed]


    row_params = (w_dt_row, dt_bias_row, jnp.swapaxes(rate_row, 1, 2), skip_row.reshape(1, share))
    params = (
        conv_taps,
        conv_bias.reshape(1, share),
        w_col_proj,
        w_dt_col,
        dt_bias_col,
        jnp.swapaxes(rate_col, 1, 2),
    )
    sent = call(
        functools.partial(pack_kernel, chips=chips),
        "pack",
        [array((2, tokens, 2 * share + width))] * chips + [like(p) for p in row_params],
        [
            pltpu.VMEM(features.shape, BF16),
            pltpu.VMEM(gate_branch.shape, BF16),
            pltpu.VMEM(w_row_proj.shape, BF16),
            pltpu.VMEM((n_col, tokens, 2 * share + width), BF16),
            pltpu.SemaphoreType.DMA((3 + len(row_params),)),
        ],
        spot,
        scalars=1,
        far=(features, gate_branch, w_row_proj, *row_params),
    )
    sent, row_params = sent[:chips], sent[chips:]
    blocks = exchange(sent)
    scratch = [
        pltpu.VMEM((line, rows, share), F32),
        pltpu.VMEM((line, rows, share), F32),
        pltpu.VMEM((line, rows, width), F32),
        pltpu.VMEM((line * rows, 2 * state), BF16),
        pltpu.VMEM((line, rows, share), F32),
    ]
    upper, tail, wide, rates, pick, got = call(
        functools.partial(upper_kernel, sources=n_col),
        "upper_rows",
        [
            array((line, rows, share)),
            array((2, line, share)),
            array((width, 2 * share)),
            array((state, rows, share), F32),
            array((state, 2 * state, 2 * LANES)),
            array((line, rows, 2 * share + width)),
        ],
        scratch,
        spot,
        *blocks,
        *row_params,
        scalars=1,
    )
    above = lax.ppermute(tail, "row", [(i, (i + 1) % n_row) for i in range(n_row)])
    lower, *params = call(
        functools.partial(lower_kernel, rank=w_dt_row.shape[1]),
        "lower_rows",
        [array((line, rows, share))] + [like(p) for p in params],
        scratch + [pltpu.SemaphoreType.DMA((len(params),))],
        near(got),
        row_params[1],
        row_params[3],
        near(wide),
        near(rates),
        near(pick),
        far=params,
    )
    sent = call(
        conv_kernel,
        "conv",
        [array((2, tokens, share))] * chips,
        [pltpu.VMEM((line + 2, rows + 8, share), F32)],
        me,
        spot,
        near(lower),
        near(upper),
        near(above),
        *params[:2],
        scalars=2,
    )
    blocks = exchange(sent)
    pieces = call(
        functools.partial(turn_kernel, sources=n_col, rows=rows),
        "turn",
        [array((tokens, col_share + width))] * n_row,
        [pltpu.VMEM((n_col, tokens, share), BF16)],
        me,
        spot,
        *blocks,
        params[2],
        scalars=2,
    )
    pieces = [pieces[0]] + [
        lax.ppermute(pieces[s], "row", [(i, (i + s) % n_row) for i in range(n_row)]) for s in range(1, n_row)
    ]
    return call(
        functools.partial(col_kernel, count=n_row, rows=rows),
        "col_scan",
        jax.ShapeDtypeStruct((column, cols, col_share), BF16),
        scan_scratch(column, cols, col_share, width, state)
        + [
            pltpu.VMEM(((column + 1) * cols, width), BF16),
            pltpu.VMEM((column + 1, cols, col_share), F32),
            pltpu.VMEM((column, cols, col_share), F32),
            pltpu.VMEM((column, cols, col_share), F32),
        ],
        me,
        *[near(piece) for piece in pieces],
        *params[3:],
        scalars=1,
    )


def solution(mesh):
    return jax.shard_map(
        local,
        mesh=mesh,
        in_specs=(
            P("row", "col", None),
            P("row", "col", None),
            P(),
            P(None, None, "col"),
            P(None, "col"),
            P(None, "col", None),
            P("col"),
            P(None, None, "col"),
            P("col"),
            P(),
            P(None, None, "row"),
            P(None, "row"),
            P(None, "row", None),
        ),
        out_specs=P(None, "col", "row"),
        check_vma=False,
    )
```

```python
import functools
import math

import jax
import jax.numpy as jnp
from jax import lax
from jax.experimental import pallas as pl
from jax.experimental.pallas import tpu as pltpu
from jax.sharding import PartitionSpec as P

LANES = 128
F32 = jnp.float32
BF16 = jnp.bfloat16
LOG2E = math.log2(math.e)


def dot(a, b):
    return jnp.dot(a, b, preferred_element_type=F32)


def silu(v):
    return v / (1.0 + jnp.exp(-v))


def softplus(v):
    return jnp.maximum(v, 0.0) + jnp.log1p(jnp.exp(-jnp.abs(v)))


def shuffle(tokens, outer, inner):
    shape = (tokens, tokens)
    to = lax.broadcasted_iota(jnp.int32, shape, 0).astype(F32)
    frm = lax.broadcasted_iota(jnp.int32, shape, 1).astype(F32)
    high = jnp.floor((to + 0.5) / inner)
    wanted = jnp.where(to < outer * inner, (to - high * inner) * outer + high, to)
    return jnp.where(frm == wanted, 1.0, 0.0).astype(BF16)


def fetches(sources, targets, sems):
    copies = [pltpu.make_async_copy(s, t, sems.at[i]) for i, (s, t) in enumerate(zip(sources, targets))]
    for copy in copies:
        copy.start()
    return copies


def shifts(chips):
    return [0, *([chips - 1] if chips > 1 else []), *range(1, chips - 1)]


def there(spot, shift):
    return spot // 2 ^ shift


def place(spot, shift, other):
    return there(spot, shift) * 2 + (spot % 2 ^ other)


def pack_kernel(spot_ref, feat_hbm, gate_hbm, w_hbm, *refs, chips):
    count = (len(refs) - 5 - chips) // 2
    param_refs, held_refs = refs[:count], refs[count + chips : 2 * count + chips]
    send_refs = refs[count : count + chips]
    feat_ref, gate_ref, w_ref, out_ref, sems = refs[2 * count + chips :]
    copies = fetches((feat_hbm, w_hbm, gate_hbm, *param_refs), (feat_ref, w_ref, gate_ref, *held_refs), sems)
    rows, cols, channels = feat_ref.shape
    tokens = rows * cols
    parts = out_ref.shape[0]
    share = channels // parts
    order = shuffle(tokens, cols, rows)
    copies[0].wait()
    feats = feat_ref[...].reshape(tokens, channels)
    moved = dot(order, feats).astype(BF16)
    for part in range(parts):
        out_ref[part, :, :share] = moved[:, part * share : (part + 1) * share]
    copies[1].wait()
    proj = dot(order, dot(feats, w_ref[...]).astype(BF16)).astype(BF16)
    for part in range(parts):
        out_ref[part, :, 2 * share :] = proj
    copies[2].wait()
    moved = dot(order, gate_ref[...].reshape(tokens, channels)).astype(BF16)
    for part in range(parts):
        out_ref[part, :, share : 2 * share] = moved[:, part * share : (part + 1) * share]
    for shift, send_ref in zip(shifts(chips), send_refs):
        for other in range(2):
            send_ref[other] = out_ref[place(spot_ref[0], shift, other)]
    for copy in copies[3:]:
        copy.wait()


def gathered(spot, refs, put):
    chips = len(refs) // 2
    for at, shift in enumerate(shifts(chips)):
        for other in range(2):
            put(place(spot, shift, other), refs[other * chips + at][other])


def one_hot(height, width, hit):
    row = lax.broadcasted_iota(jnp.int32, (height, width), 0)
    column = lax.broadcasted_iota(jnp.int32, (height, width), 1)
    return jnp.where(hit(row, column), 1.0, 0.0).astype(BF16)


def prepare(proj, w_dt_ref, bias_ref, rate_ref, wide_ref, step_ref, rates_ref, pick_ref, ends_ref):
    _, rank, channels = w_dt_ref.shape
    state = rate_ref.shape[1]
    segment = rank + 2 * state
    lines = rates_ref.shape[2]
    wide_ref[...] = jnp.zeros_like(wide_ref)
    for k in range(2):
        wide_ref[pl.ds(k * segment, rank), pl.ds(k * channels, channels)] = w_dt_ref[k]
    raw = dot(proj, wide_ref[...])
    for k in range(2):
        part = raw[:, k * channels : (k + 1) * channels] + bias_ref[k : k + 1, :]
        step_ref[k] = softplus(part).reshape(step_ref.shape[1:])
        turned = rate_ref[k] * -LOG2E
        for n in range(state):
            rates_ref[k, n] = jnp.broadcast_to(turned[n : n + 1, :], (lines, channels))
        base = k * segment + rank
        ends_ref[k] = dot(proj, one_hot(proj.shape[1], 2 * state, lambda r, c: r == c + base)).astype(BF16)
    for n in range(state):
        pick_ref[n] = one_hot(2 * state, 2 * LANES, lambda r, c: r == n + jnp.where(c < LANES, 0, state))


def scan(step_ref, value_ref, rates_ref, pick_ref, ends_ref, state_ref, out_ref, back_ref):
    positions, lines, channels = out_ref.shape
    state = rates_ref.shape[1]
    width = min(channels, LANES)
    groups = [pl.ds(at, width) for at in range(0, channels, width)]
    size = math.gcd(positions, max(1, 32 // (lines * len(groups))))
    blocks = positions // size
    state_ref[...] = jnp.zeros_like(state_ref)

    def advance(at, _):
        firsts = (pl.multiple_of(at * size, size), pl.multiple_of((blocks - 1 - at) * size, size))
        orders = (list(range(size)), list(reversed(range(size))))
        steps, drives, ends = [], [], []
        for k, first in enumerate(firsts):
            steps.append([[step_ref[k, first + p, :, g] for g in groups] for p in range(size)])
            drives.append([[steps[k][p][i] * value_ref[first + p, :, g] for i, g in enumerate(groups)] for p in range(size)])
            ends.append(ends_ref[k, pl.ds(pl.multiple_of(first * lines, size * lines), size * lines), :])
        totals = [[[None] * len(groups) for _ in range(size)] for _ in firsts]
        both = jnp.concatenate(ends, axis=0)
        for n in range(state):
            spread = dot(both, pick_ref[n])
            held = [[state_ref[k, n, :, g] for g in groups] for k in range(2)]
            rates = [[rates_ref[k, n, :, g] for g in groups] for k in range(2)]
            for at_p in range(size):
                for k in range(2):
                    p = orders[k][at_p]
                    row = (k * size + p) * lines
                    b = spread[row : row + lines, :width]
                    c = spread[row : row + lines, LANES : LANES + width]
                    for i in range(len(groups)):
                        held[k][i] = jnp.exp2(steps[k][p][i] * rates[k][i]) * held[k][i] + drives[k][p][i] * b
                        read = c * held[k][i]
                        totals[k][p][i] = read if n == 0 else totals[k][p][i] + read
            for k in range(2):
                for i, g in enumerate(groups):
                    state_ref[k, n, :, g] = held[k][i]
        for p in range(size):
            for i, g in enumerate(groups):
                out_ref[firsts[0] + p, :, g] = totals[0][p][i]
                back_ref[firsts[1] + p, :, g] = totals[1][p][i]
        return 0

    lax.fori_loop(0, blocks, advance, 0, unroll=True)


def joint_scan(step_ref, value_ref, rates_ref, pick_ref, ends_ref, out_ref):
    positions, lines, channels = out_ref.shape
    state = rates_ref.shape[0]
    size = math.gcd(positions, 16)
    held = [jnp.zeros((lines, channels), F32)] * state
    for first in range(0, positions, size):
        steps = [step_ref[first + p] for p in range(size)]
        drives = [steps[p] * value_ref[first + p] for p in range(size)]
        totals = [None] * size
        ends = ends_ref[first * lines : (first + size) * lines, :]
        for n in range(state):
            spread = dot(ends, pick_ref[n])
            rates = rates_ref[n]
            for p in range(size):
                b = spread[p * lines : (p + 1) * lines, :channels]
                c = spread[p * lines : (p + 1) * lines, LANES : LANES + channels]
                held[n] = jnp.exp2(steps[p] * rates) * held[n] + drives[p] * b
                read = c * held[n]
                totals[p] = read if n == 0 else totals[p] + read
        for p in range(size):
            out_ref[first + p] = totals[p]


def row_tables(w_dt_ref, rate_ref, wide_ref, rates_ref, pick_ref):
    _, rank, channels = w_dt_ref.shape
    state = rate_ref.shape[1]
    segment = rank + 2 * state
    lines = rates_ref.shape[1]
    low = lax.broadcasted_iota(jnp.int32, (lines, channels), 0) < lines // 2
    wide_ref[...] = jnp.zeros_like(wide_ref)
    for k in range(2):
        wide_ref[pl.ds(k * segment, rank), pl.ds(k * channels, channels)] = w_dt_ref[k]
    turned = [rate_ref[k] * -LOG2E for k in range(2)]
    for n in range(state):
        rates_ref[n] = jnp.where(low, *[jnp.broadcast_to(t[n : n + 1, :], (lines, channels)) for t in turned])
        pick_ref[n] = one_hot(2 * state, 2 * LANES, lambda r, c: r == n + jnp.where(c < LANES, 0, state))


def half_rows(upper, rank, got_ref, bias_ref, skip_ref, wide_ref, rates_ref, pick_ref, out_ref, scratch):
    step_ref, value_ref, proj_ref, ends_ref, sum_ref = scratch
    positions, lines, share = out_ref.shape
    state = rates_ref.shape[0]
    segment = rank + 2 * state
    width = proj_ref.shape[2]
    half = lines // 2

    def low(columns):
        return lax.broadcasted_iota(jnp.int32, (lines, columns), 0) < half

    def swap(v):
        return pltpu.roll(v, half, 0)

    def packed(p, at):
        there = got_ref[p, :, at].astype(F32)
        back = got_ref[positions - 1 - p, :, at].astype(F32)
        there, back = (swap(there), back) if upper else (there, swap(back))
        return jnp.where(low(there.shape[1]), there, back)

    for p in range(positions):
        value_ref[p] = packed(p, pl.ds(0, share))
        proj_ref[p] = packed(p, pl.ds(2 * share, width))
    proj = proj_ref[...].reshape(positions * lines, width).astype(BF16)
    raw = dot(proj, wide_ref[...])
    parts = [(raw[:, k * share : (k + 1) * share] + bias_ref[k : k + 1, :]).reshape(positions, lines, share) for k in range(2)]
    step_ref[...] = softplus(jnp.where(low(share), *parts))
    ends = [
        dot(proj, one_hot(width, 2 * state, lambda r, c: r == c + k * segment + rank)).reshape(positions, lines, 2 * state)
        for k in range(2)
    ]
    ends_ref[...] = jnp.where(low(2 * state), *ends).reshape(ends_ref.shape).astype(BF16)
    joint_scan(step_ref, value_ref, rates_ref, pick_ref, ends_ref, sum_ref)
    for p in range(positions):
        there, back = sum_ref[p], sum_ref[positions - 1 - p]
        mix = swap(there) + back if upper else there + swap(back)
        mix = mix + skip_ref[...] * got_ref[p, :, :share].astype(F32)
        gated = mix * silu(got_ref[p, :, share : 2 * share].astype(F32))
        value_ref[p] = gated
        out_ref[p] = gated.astype(BF16)


def upper_kernel(spot_ref, *refs, sources):
    block_refs, (w_dt_ref, bias_ref, rate_ref, skip_ref), refs = refs[:sources], refs[sources : sources + 4], refs[sources + 4 :]
    out_ref, tail_ref, wide_ref, rates_ref, pick_ref, got_ref, *scratch = refs
    positions, lines, share = out_ref.shape
    cols = positions // sources

    def put(source, block):
        got_ref[pl.ds(source * cols, cols)] = block.reshape(cols, lines, block.shape[1])

    gathered(spot_ref[0], block_refs, put)
    row_tables(w_dt_ref, rate_ref, wide_ref, rates_ref, pick_ref)
    half_rows(True, w_dt_ref.shape[1], got_ref, bias_ref, skip_ref, wide_ref, rates_ref, pick_ref, out_ref, scratch)
    flat_ref = scratch[1].reshape(positions * lines, share)
    for j in range(2):
        tail_ref[j] = flat_ref[pl.ds(lines - 2 + j, positions, stride=lines), :].astype(BF16)


def lower_kernel(got_ref, bias_ref, skip_ref, wide_ref, rates_ref, pick_ref, *refs, rank):
    *scratch, sems = refs[-6:]
    count = (len(refs) - 7) // 2
    out_ref, *held_refs = refs[count:-6]
    copies = fetches(refs[:count], held_refs, sems)
    half_rows(False, rank, got_ref, bias_ref, skip_ref, wide_ref, rates_ref, pick_ref, out_ref, scratch)
    for copy in copies:
        copy.wait()


def conv_kernel(me_ref, spot_ref, lower_ref, upper_ref, above_ref, taps_ref, bias_ref, *refs):
    *send_refs, pad_ref = refs
    positions, lines, share = lower_ref.shape
    cols = positions // (2 * len(send_refs))
    height = pad_ref.shape[1]
    top = height - lines
    zero_edge = jnp.zeros((1, height, share), F32)
    pad_ref[0:1] = zero_edge
    pad_ref[positions + 1 : positions + 2] = zero_edge
    slot = lax.broadcasted_iota(jnp.int32, (lines, share), 0)
    mid = jnp.where(slot < lines // 2, lower_ref[...].astype(F32), upper_ref[...].astype(F32))
    pad_ref[1 : positions + 1, top:, :] = mid
    flat_ref = pad_ref.reshape((positions + 2) * height, share)
    for j in range(2):
        flat_ref[pl.ds(height + top - 2 + j, positions, stride=height), :] = above_ref[j].astype(F32)
    first = me_ref[0] == 0
    beyond = (jnp.logical_and(first, slot == 1), None, jnp.logical_and(first, slot == 0))
    taps = []
    for i in range(3):
        wide = [jnp.broadcast_to(taps_ref[i, j : j + 1, :], (lines, share)) for j in range(3)]
        taps.append(wide if beyond[i] is None else [jnp.where(beyond[i], 0.0, tap) for tap in wide])
    bias = jnp.broadcast_to(bias_ref[...], (lines, share))

    spot = spot_ref[0]
    for shift, send_ref in zip(shifts(len(send_refs)), send_refs):
        for other in range(2):
            start = place(spot, shift, other) * cols
            for w in range(cols):
                total = bias
                for i in range(3):
                    for j in range(3):
                        total = total + taps[i][j] * pad_ref[start + w + j, top - 2 + i : top - 2 + i + lines, :]
                send_ref[other, w * lines : (w + 1) * lines, :] = silu(total).astype(BF16)


def turn_kernel(me_ref, spot_ref, *refs, sources, rows):
    block_refs, w_ref, out_refs, got_ref = refs[:sources], refs[sources], refs[sources + 1 : -1], refs[-1]
    parts, tokens, share = got_ref.shape
    width = w_ref.shape[1]
    count = len(out_refs)
    each = parts // count
    order = shuffle(tokens, rows, tokens // rows)
    sums = []

    def put(source, block):
        got_ref[source] = block
        sums.append(dot(block, w_ref[pl.ds(pl.multiple_of(source * share, share), share), :]))

    gathered(spot_ref[0], block_refs, put)
    proj = dot(order, sum(sums).astype(BF16)).astype(BF16)
    me = me_ref[0]
    for shift in range(count):
        to = lax.rem(me + shift, count)
        for j in range(each):
            moved = dot(order, got_ref[to * each + j]).astype(BF16)
            out_refs[shift][:, j * share : (j + 1) * share] = moved
        out_refs[shift][:, each * share :] = proj


def col_kernel(
    me_ref, *refs, count, rows,
):
    got_refs = refs[:count]
    (w_dt_ref, bias_ref, rate_ref, out_ref, wide_ref, step_ref, rates_ref, pick_ref, ends_ref,
     state_ref, proj_ref, value_ref, sum_ref, back_ref) = refs[count:]
    positions, lines, share = out_ref.shape
    block = rows * lines
    me = me_ref[0]
    for shift in range(count):
        frm = lax.rem(me + count - shift, count)
        piece = got_refs[shift][:, :share].astype(F32).reshape(rows, lines, share)
        value_ref[pl.ds(frm * rows, rows)] = piece
        proj_ref[pl.ds(pl.multiple_of(frm * block, block), block), :] = got_refs[shift][:, share:]

        @pl.when(frm == 0)
        def _():
            value_ref[positions] = piece[0]
            proj_ref[pl.ds(positions * lines, lines), :] = got_refs[shift][:lines, share:]

    proj = proj_ref[lines:, :]
    prepare(proj, w_dt_ref, bias_ref, rate_ref, wide_ref, step_ref, rates_ref, pick_ref, ends_ref)
    values = value_ref.at[pl.ds(1, positions)]
    scan(step_ref, values, rates_ref, pick_ref, ends_ref, state_ref, sum_ref, back_ref)
    out_ref[...] = (sum_ref[...] + back_ref[...]).astype(BF16)


def vmem():
    return pl.BlockSpec(memory_space=pltpu.VMEM)


def smem():
    return pl.BlockSpec(memory_space=pltpu.SMEM)


def call(kernel, name, outs, scratch, *args, scalars=0, far=()):
    many = isinstance(outs, (list, tuple))
    hbm = pl.BlockSpec(memory_space=pltpu.HBM)
    return pl.pallas_call(
        kernel,
        name=name,
        out_shape=outs,
        in_specs=[smem()] * scalars + [vmem()] * (len(args) - scalars) + [hbm] * len(far),
        out_specs=[vmem()] * len(outs) if many else vmem(),
        scratch_shapes=scratch,
        compiler_params=pltpu.CompilerParams(vmem_limit_bytes=24 << 20),
    )(*args, *[pltpu.with_memory_space_constraint(x, pltpu.HBM) for x in far])


def array(shape, dtype=BF16):
    return pltpu.VMEM(shape, dtype)


def near(x):
    return pltpu.with_memory_space_constraint(x, pltpu.VMEM)


def like(x):
    return array(x.shape, x.dtype)


def scan_scratch(positions, lines, channels, width, state):
    return [
        pltpu.VMEM((width, 2 * channels), BF16),
        pltpu.VMEM((2, positions, lines, channels), F32),
        pltpu.VMEM((2, state, lines, channels), F32),
        pltpu.VMEM((state, 2 * state, 2 * LANES), BF16),
        pltpu.VMEM((2, positions * lines, 2 * state), BF16),
        pltpu.VMEM((2, state, lines, channels), F32),
    ]


def local(
    features, gate_branch, w_row_proj, w_dt_row, dt_bias_row, rate_row, skip_row,
    conv_taps, conv_bias, w_col_proj, w_dt_col, dt_bias_col, rate_col,
):
    rows, cols, channels = features.shape
    width = w_row_proj.shape[1]
    state = rate_row.shape[2]
    n_col, n_row = lax.axis_size("col"), lax.axis_size("row")
    share, col_share = channels // n_col, channels // n_row
    line, column = cols * n_col, rows * n_row
    tokens = rows * cols
    me = lax.axis_index("row").astype(jnp.int32).reshape(1)
    spot = lax.axis_index("col").astype(jnp.int32).reshape(1)
    chips = n_col // 2

    def exchange(pieces):
        pieces = [pieces[0]] + [
            lax.ppermute(piece, "col", [(i, place(i, s, 0)) for i in range(n_col)])
            for s, piece in list(zip(shifts(chips), pieces))[1:]
        ]
        passed = [lax.ppermute(piece, "col", [(i, i ^ 1) for i in range(n_col)]) for piece in pieces]
        return [near(piece) for piece in pieces + passed]


    row_params = (w_dt_row, dt_bias_row, jnp.swapaxes(rate_row, 1, 2), skip_row.reshape(1, share))
    params = (
        conv_taps,
        conv_bias.reshape(1, share),
        w_col_proj,
        w_dt_col,
        dt_bias_col,
        jnp.swapaxes(rate_col, 1, 2),
    )
    sent = call(
        functools.partial(pack_kernel, chips=chips),
        "pack",
        [array((2, tokens, 2 * share + width))] * chips + [like(p) for p in row_params],
        [
            pltpu.VMEM(features.shape, BF16),
            pltpu.VMEM(gate_branch.shape, BF16),
            pltpu.VMEM(w_row_proj.shape, BF16),
            pltpu.VMEM((n_col, tokens, 2 * share + width), BF16),
            pltpu.SemaphoreType.DMA((3 + len(row_params),)),
        ],
        spot,
        scalars=1,
        far=(features, gate_branch, w_row_proj, *row_params),
    )
    sent, row_params = sent[:chips], sent[chips:]
    blocks = exchange(sent)
    scratch = [
        pltpu.VMEM((line, rows, share), F32),
        pltpu.VMEM((line, rows, share), F32),
        pltpu.VMEM((line, rows, width), F32),
        pltpu.VMEM((line * rows, 2 * state), BF16),
        pltpu.VMEM((line, rows, share), F32),
    ]
    upper, tail, wide, rates, pick, got = call(
        functools.partial(upper_kernel, sources=n_col),
        "upper_rows",
        [
            array((line, rows, share)),
            array((2, line, share)),
            array((width, 2 * share)),
            array((state, rows, share), F32),
            array((state, 2 * state, 2 * LANES)),
            array((line, rows, 2 * share + width)),
        ],
        scratch,
        spot,
        *blocks,
        *row_params,
        scalars=1,
    )
    above = lax.ppermute(tail, "row", [(i, (i + 1) % n_row) for i in range(n_row)])
    lower, *params = call(
        functools.partial(lower_kernel, rank=w_dt_row.shape[1]),
        "lower_rows",
        [array((line, rows, share))] + [like(p) for p in params],
        scratch + [pltpu.SemaphoreType.DMA((len(params),))],
        near(got),
        row_params[1],
        row_params[3],
        near(wide),
        near(rates),
        near(pick),
        far=params,
    )
    sent = call(
        conv_kernel,
        "conv",
        [array((2, tokens, share))] * chips,
        [pltpu.VMEM((line + 2, rows + 8, share), F32)],
        me,
        spot,
        near(lower),
        near(upper),
        near(above),
        *params[:2],
        scalars=2,
    )
    blocks = exchange(sent)
    pieces = call(
        functools.partial(turn_kernel, sources=n_col, rows=rows),
        "turn",
        [array((tokens, col_share + width))] * n_row,
        [pltpu.VMEM((n_col, tokens, share), BF16)],
        me,
        spot,
        *blocks,
        params[2],
        scalars=2,
    )
    pieces = [pieces[0]] + [
        lax.ppermute(pieces[s], "row", [(i, (i + s) % n_row) for i in range(n_row)]) for s in range(1, n_row)
    ]
    return call(
        functools.partial(col_kernel, count=n_row, rows=rows),
        "col_scan",
        jax.ShapeDtypeStruct((column, cols, col_share), BF16),
        scan_scratch(column, cols, col_share, width, state)
        + [
            pltpu.VMEM(((column + 1) * cols, width), BF16),
            pltpu.VMEM((column + 1, cols, col_share), F32),
            pltpu.VMEM((column, cols, col_share), F32),
            pltpu.VMEM((column, cols, col_share), F32),
        ],
        me,
        *[near(piece) for piece in pieces],
        *params[3:],
        scalars=1,
    )


def solution(mesh):
    return jax.shard_map(
        local,
        mesh=mesh,
        in_specs=(
            P("row", "col", None),
            P("row", "col", None),
            P(),
            P(None, None, "col"),
            P(None, "col"),
            P(None, "col", None),
            P("col"),
            P(None, None, "col"),
            P("col"),
            P(),
            P(None, None, "row"),
            P(None, "row"),
            P(None, "row", None),
        ),
        out_specs=P(None, "col", "row"),
        check_vma=False,
    )
```
